512 devices in a mesh: space: 128 (over x, z, core), mem: 4 (over y).
Axes of the slice: x: 4, y: 4, z: 16, core: 2. Of those that a mesh axis runs over, the one named last changes fastest.
Arguments:
- state: float32 [64, 3, 2048, 256], P('mem', None, 'space'), may hold values from -6 to 6
- depth: float32 [2048, 256], P('space'), may hold values from 0.5 to 2
- obs_cells: int32 [4, 8192, 128], P(None, 'space'), may hold values from 0 to 4095, as said below
- obs_weights: float32 [4, 8192, 128], P(None, 'space'), may hold values from 0 to 0.5
- owner_map: int32 [8192, 1], P('space'), may hold values from 0 to 127; in each aligned block of 64 rows (0 to 63, 64 to 127, ...) at most 2 rows name the same one
- obs_values: float32 [128, 128, 2, 128], P('space'), may hold values from -8 to 8
- obs_precision: float32 [128, 128, 2, 128], P('space'), may hold values from 0.5 to 6
Outputs:
- analysis: float32 [64, 3, 2048, 256], P('mem', None, 'space')
The draws below stay inside these ranges and needn't reach their ends.
Inputs may be any that keep to these rules, and one draw needn't show every extreme that they name: The cells of block b lie in the rows of space device b // 64; obs_cells is the offset within those rows. `owner_map`: among the 64 blocks of one space device no owner is named more than 2 times, and in some device one owner is named exactly 2 times.
All inputs are finite; a program needn't handle non-finite values.
Results may differ from the reference program's by a relative error of at most 0.00012.
Values sent between devices are 32-bit elements; how exact they have to be, the bound alone decides.
A program may use at most 64 MiB of HBM per device.

```python
import math
import jax
import jax.numpy as jnp
import numpy as np
from jax import lax

M = 64
CX = 16
NY = 256
STEPS = 2
OBS_BLK = 128
SRC_BLK = 64
PAIR_CAP = 2
NX = 2048
BLOCKS = 8192
N_SPACE = 128


def draw_obs_cells(key, part):
    strip = CX * NY
    offsets = jax.random.randint(key, (4, BLOCKS, OBS_BLK), 0, strip)
    offsets = offsets.at[0, 0, 0].set(0)
    offsets = offsets.at[3, BLOCKS - 1, OBS_BLK - 1].set(strip - 1)
    return offsets.astype(jnp.int32)


def draw_obs_precision(key, part):
    shape = (N_SPACE, N_SPACE, PAIR_CAP, OBS_BLK)
    source = jnp.arange(N_SPACE, dtype=jnp.float32)[None, :, None, None] / max(N_SPACE - 1, 1)
    base = jnp.exp(jax.random.uniform(key, shape, jnp.float32, math.log(0.5), math.log(2.0)))
    ramp = 1.0 + 2.0 * source
    return (base * ramp).astype(jnp.float32)


def level_of(own_key, extent, split, low, top_value):
    def one(position, shards_of):
        draws = jax.random.uniform(jax.random.fold_in(jax.random.fold_in(own_key, 6), position), (shards_of,), jnp.float32, low / len(split), top_value / len(split))
        return jnp.repeat(jnp.exp(draws), extent[position] // shards_of).reshape((-1,) + (1,) * (len(extent) - position - 1))

    factor_of = one(*split[0])
    for cut in split[1:]:
        factor_of = factor_of * one(*cut)
    return factor_of


def assign_block(stream_key, own, number, rows, amount, top, limit, slope):
    sequence = jax.random.permutation(stream_key, amount)
    packed, ordinary = load_shares(amount, rows * top, limit, slope, True), load_shares(amount, rows * top, limit, slope, False)
    places = jnp.arange(amount)

    def named(lengths, rotation):
        used = int((lengths > 0).sum())
        fixed = max(1, used // 4)
        moved = fixed + (places - fixed + rotation * (used - fixed)) % max(1, amount - fixed)
        return jnp.zeros((amount,), jnp.int32).at[sequence[jnp.where(places < fixed, places, moved)]].set(jnp.asarray(lengths, jnp.int32))

    lengths = jnp.where(number % 4 == 0, named(packed, number // 4), named(ordinary, number - number // 4 - 1))
    mixed = jax.random.permutation(jax.random.fold_in(own, 3), amount)
    source_of, taker = mixed[0:amount // 2 * 2:2], mixed[1:amount // 2 * 2:2]
    margin = jnp.minimum(lengths[source_of] - 1, limit - lengths[taker]) // 2
    margin = jnp.where((source_of == sequence[0]) | (taker == sequence[0]) | (lengths[taker] == 0), 0, jnp.maximum(margin, 0))
    moved = jax.random.randint(jax.random.fold_in(own, 4), (amount // 2,), 0, 1 << 20) % (margin + 1)
    lengths = lengths.at[source_of].add(-moved).at[taker].add(moved)
    labels = jnp.searchsorted(jnp.cumsum(lengths), jnp.arange(rows * top), side="right").astype(jnp.int32)
    grid = labels.reshape(top, rows).T
    grid = grid[jax.random.permutation(jax.random.fold_in(own, 1), rows)]
    rotation = jax.random.randint(jax.random.fold_in(own, 2), (rows, 1), 0, top)
    return jnp.take_along_axis(grid, (jnp.arange(top)[None, :] + rotation) % top, axis=1)


def load_shares(number_of, total, reach, lean, full):
    portions = [(1 << 20) // math.isqrt(grade ** lean) + 1 for grade in range(1, number_of + 1)]
    largest = reach if full else min(reach, max(-(-total // number_of), total * portions[0] // sum(portions)))
    least = 1 if total - largest >= number_of - 1 else 0
    holding, spare = [largest] + [least] * (number_of - 1), total - largest - least * (number_of - 1)
    while spare > 0:
        free = [i for i in range(1, number_of) if holding[i] < largest] or [i for i in range(1, number_of) if holding[i] < reach]
        mass, left = sum([portions[i] for i in free]), spare
        for i in free:
            more = min(reach - holding[i], max(1, left * portions[i] // mass), spare)
            holding[i] = holding[i] + more
            spare = spare - more
    return np.array(holding)


def centred(own_key, extent, width, most, shards=(), kind=jnp.bfloat16):
    drawn = width * jax.random.normal(own_key, extent, jnp.float32)
    if shards:
        drawn = drawn * level_of(own_key, extent, shards, -0.22, 0.18)
    return jnp.clip(drawn, -most, most).astype(kind)


def setup_inputs(seed: int = 0) -> dict:
    key_list = jax.random.split(jax.random.key(seed), 8)
    state = centred(key_list[0], (M, 3, NX, NY), 1.0, 6.0, ((0, 4), (2, 128)), jnp.float32)
    depth = jnp.clip(jnp.exp(math.log(2.0) - 1.3862944 * jax.random.uniform(key_list[1], (NX, NY), jnp.float32) ** level_of(key_list[1], (NX, NY), ((0, 128),), -0.2, 0.2)), 0.5, 2.0)
    obs_cells = draw_obs_cells(jax.random.fold_in(key_list[7], 71), 0)
    obs_weights = jnp.clip(0.5 * jax.random.uniform(key_list[3], (4, BLOCKS, OBS_BLK), jnp.float32) ** level_of(key_list[3], (4, BLOCKS, OBS_BLK), ((1, 128),), -0.2, 0.2), 0.0, 0.5)
    owner_map_keys = jax.random.split(jax.random.fold_in(key_list[4], 1), BLOCKS // SRC_BLK)
    owner_map_turns = jax.random.permutation(jax.random.fold_in(key_list[4], 3), BLOCKS // SRC_BLK)
    owner_map = jax.vmap(lambda own, number: assign_block(jax.random.fold_in(key_list[4], 2), own, number, SRC_BLK, N_SPACE, 1, PAIR_CAP, 2))(owner_map_keys, owner_map_turns).reshape((BLOCKS, 1))
    obs_values = centred(key_list[5], (N_SPACE, N_SPACE, PAIR_CAP, OBS_BLK), 1.5, 8.0, ((0, 128),), jnp.float32)
    obs_precision = draw_obs_precision(jax.random.fold_in(key_list[7], 71), 0)
    return {"state": state, "depth": depth, "obs_cells": obs_cells, "obs_weights": obs_weights, "owner_map": owner_map, "obs_values": obs_values, "obs_precision": obs_precision}


mass_rate = 0.2
wave_rate = 0.2
turn_rate = 0.1

def diff_rows(field):
    widths = [(0, 0)] * (field.ndim - 2) + [(1, 1), (0, 0)]
    padded = jnp.pad(field, widths)
    return padded[..., 2:, :] - padded[..., :-2, :]

def diff_cols(field):
    return jnp.roll(field, -1, axis=-1) - jnp.roll(field, 1, axis=-1)

def advance(fluid_elevation, zonal_wind, meridional_wind, depth, inside):
    fluid_elevation = (fluid_elevation - mass_rate * (diff_rows(depth * zonal_wind) + diff_cols(depth * meridional_wind))) * inside
    east_new = (zonal_wind - wave_rate * diff_rows(fluid_elevation) + turn_rate * meridional_wind) * inside
    north_new = (meridional_wind - wave_rate * diff_cols(fluid_elevation) - turn_rate * zonal_wind) * inside
    return (fluid_elevation, east_new, north_new)

def gram_terms(values, seen, weight, scale):
    middle = lax.optimization_barrier(jnp.mean(values, axis=0))
    factor = weight * scale
    scaled = (values - middle[None]) * factor[None]
    depart = (seen - middle) * factor
    gram = jnp.einsum('mrk,nrk->mn', scaled, scaled, precision=lax.Precision.HIGHEST)
    proj = jnp.einsum('mrk,rk->m', scaled, depart, precision=lax.Precision.HIGHEST)
    return (gram, proj)

def make_mixing(lower, proj, members):
    eye = jnp.eye(members, dtype=jnp.float32)
    first = lax.linalg.triangular_solve(lower, proj[:, None], left_side=True, lower=True)
    mean_weights = lax.linalg.triangular_solve(lower, first, left_side=True, lower=True, transpose_a=True)[:, 0]
    inverse_lower = lax.linalg.triangular_solve(lower, eye, left_side=True, lower=True)
    spread = math.sqrt(members - 1) * inverse_lower.T
    coef = mean_weights[:, None] + spread
    return coef + (1.0 - lax.optimization_barrier(jnp.sum(coef, axis=0)))[None, :] / members

def block_slots(owners):
    same = (owners[:, :, None] == owners[:, None, :]).astype(jnp.int32)
    order = jnp.arange(owners.shape[1], dtype=jnp.int32)
    earlier = (order[:, None] < order[None, :]).astype(jnp.int32)
    return lax.optimization_barrier(jnp.sum(same * earlier[None], axis=1))

def reference(state, depth, obs_cells, obs_weights, owner_map, obs_values, obs_precision):
    fluid_elevation, zonal_wind, meridional_wind = (state[:, 0], state[:, 1], state[:, 2])
    for step in range(STEPS):
        fluid_elevation, zonal_wind, meridional_wind = advance(fluid_elevation, zonal_wind, meridional_wind, depth, jnp.float32(1.0))
    prior_fields = jnp.stack([fluid_elevation, zonal_wind, meridional_wind], axis=1)
    flat = fluid_elevation.reshape(M, NX * NY)
    source = jnp.arange(BLOCKS, dtype=jnp.int32) // SRC_BLK
    cells = (obs_cells + (source * (CX * NY))[None, :, None]).astype(jnp.int32)

    def predict(row):
        return lax.optimization_barrier(jnp.sum(obs_weights * row[cells], axis=0))
    predicted = lax.map(predict, flat)
    owners = owner_map[:, 0]
    slots = block_slots(owners.reshape(N_SPACE, SRC_BLK)).reshape(BLOCKS)
    seen = obs_values[owners, source, slots]
    weight = obs_precision[owners, source, slots]
    scale = math.sqrt((M - 1) / (BLOCKS * OBS_BLK))
    gram, proj = gram_terms(predicted, seen, weight, scale)
    system = (M - 1) * jnp.eye(M, dtype=jnp.float32) + gram
    lower = jnp.linalg.cholesky(system)
    transform_weights = make_mixing(lower, proj, M)
    return jnp.einsum('gv,gpbo->vpbo', transform_weights, prior_fields, precision=lax.Precision.HIGHEST)
```

```python
import math

import jax
import jax.numpy as jnp
from jax import lax
from jax.experimental import pallas as pl
from jax.experimental.pallas import tpu as pltpu
from jax.sharding import PartitionSpec as P

M = 64
NS = 128
NM = 4
NZ = 16
GROUP = 32
LM = M // NM
ROWS = 16
COLS = 256
HALO = 4
EXT = ROWS + 2 * HALO
BLK = 16
OBS = 128
N_OBS = 8192 * 128
MESH = pl.DeviceIdType.MESH
HIGHEST = lax.Precision.HIGHEST
mass_rate = 0.2
wave_rate = 0.2
turn_rate = 0.1


def east(field):
    return pltpu.roll(field, COLS - 1, 1)


def west(field):
    return pltpu.roll(field, 1, 1)


def forecast_heights(s, S, DB, H1, U1, V1, H2):
    inside_low = jnp.where(s > 0, 1.0, 0.0).astype(jnp.float32)
    inside_high = jnp.where(s < NS - 1, 1.0, 0.0).astype(jnp.float32)

    def inside(i):
        return jnp.where(i < HALO, inside_low, jnp.where(i >= HALO + ROWS, inside_high, 1.0))

    groups = [slice(0, 8), slice(8, 16)]
    for i in range(HALO):
        DB[i] = DB[i] * inside_low
        DB[HALO + ROWS + i] = DB[HALO + ROWS + i] * inside_high

    @pl.loop(1, EXT - 1)
    def _(i):
        keep = inside(i)
        for g in groups:
            flux = DB[i] * S[2, i, g]
            change = DB[i + 1] * S[1, i + 1, g] - DB[i - 1] * S[1, i - 1, g] + (east(flux) - west(flux))
            H1[i, g] = (S[0, i, g] - mass_rate * change) * keep

    @pl.loop(2, EXT - 2)
    def _(i):
        for g in groups:
            u, v, h = S[1, i, g], S[2, i, g], H1[i, g]
            U1[i, g] = u - wave_rate * (H1[i + 1, g] - H1[i - 1, g]) + turn_rate * v
            V1[i, g] = v - wave_rate * (east(h) - west(h)) - turn_rate * u

    @pl.loop(3, EXT - 3)
    def _(i):
        keep = inside(i)
        for g in groups:
            flux = DB[i] * V1[i, g]
            change = DB[i + 1] * U1[i + 1, g] - DB[i - 1] * U1[i - 1, g] + (east(flux) - west(flux))
            H2[i, g] = (H1[i, g] - mass_rate * change) * keep


def pack_block(yb, fc, packed, inverse):
    top = lax.fori_loop(
        0, ROWS, lambda r, t: jnp.maximum(t, jnp.abs(fc[yb, 0, r])), jnp.zeros((LM, COLS), jnp.float32)
    )
    top = jnp.maximum(jnp.max(top, axis=1, keepdims=True), 1e-30)
    scale = 32000.0 / top
    inverse[yb] = jnp.broadcast_to(top * (1.0 / 32000.0), (LM, OBS))

    @pl.loop(0, ROWS)
    def _(r):
        q = jnp.floor(fc[yb, 0, r] * scale + 0.5).astype(jnp.int32)
        packed[yb, r] = (q[0:8] << 16) | (q[8:16] & 0xFFFF)


def interpolate(blocks, packed, inverse, cells, weights, pred):
    @pl.loop(0, BLK)
    def _(b):
        @pl.loop(0, 2)
        def _(half):
            lane, chunk, weight = [], [], []
            for k in range(2):
                cell = jnp.broadcast_to(cells[half * 2 + k, pl.ds(b, 1), :], (8, OBS))
                lane.append(cell & (OBS - 1))
                chunk.append(cell >> 7)
                weight.append(jnp.broadcast_to(weights[half * 2 + k, pl.ds(b, 1), :], (8, OBS)))
            held = [[jnp.zeros((8, OBS), jnp.int32) for _ in blocks] for _ in range(2)]
            for c in range(ROWS * COLS // OBS):
                row, col = c // 2, (c % 2) * OBS
                here = [chunk[k] == c for k in range(2)]
                for g, yb in enumerate(blocks):
                    values = packed[yb, row, :, col : col + OBS]
                    for k in range(2):
                        found = jnp.take_along_axis(values, lane[k], axis=1, mode="promise_in_bounds")
                        held[k][g] = jnp.where(here[k], found, held[k][g])
            for g, yb in enumerate(blocks):
                high = sum((held[k][g] >> 16).astype(jnp.float32) * weight[k] for k in range(2))
                low = sum(((held[k][g] << 16) >> 16).astype(jnp.float32) * weight[k] for k in range(2))
                part = jnp.concatenate([high, low], axis=0) * inverse[yb]

                @pl.when(half == 0)
                def _():
                    pred[yb, b] = part

                @pl.when(half == 1)
                def _():
                    pred[yb, b] = pred[yb, b] + part


def main_kernel(
    target, state, depth, cells_hbm, weights_hbm, values, precisions, fc, total,
    st, dp, cells, weights, S, DB, H1, U1, V1, H2, packed, inverse, pred, X, tab_v, tab_p, Gs, rs, zs, zb, ga,
    load_sem, halo_send, halo_recv, ag_send, ag_recv, tab_send, tab_recv, red_send, red_recv,
):
    s = lax.axis_index("space")
    y = lax.axis_index("mem")
    core = s % 2
    z = (s // 2) % NZ
    x = s // (2 * NZ)
    y_low, y_high, y_far = (y + 3) % NM, (y + 1) % NM, (y + 2) % NM
    place = (x * NM + y) * 2 + core

    def member_of(q):
        return ((q // 8) * (2 * NZ) + z * 2 + q % 2, (q // 2) % NM)

    loads = [
        pltpu.make_async_copy(state.at[:, pl.ds(0, OBS)], st.at[0], load_sem.at[0]),
        pltpu.make_async_copy(state.at[:, pl.ds(OBS, OBS)], st.at[1], load_sem.at[6]),
        pltpu.make_async_copy(depth, dp, load_sem.at[1]),
        pltpu.make_async_copy(cells_hbm.at[:, pl.ds(pl.multiple_of(y * BLK, BLK), BLK)], cells, load_sem.at[2]),
        pltpu.make_async_copy(weights_hbm.at[:, pl.ds(pl.multiple_of(y * BLK, BLK), BLK)], weights, load_sem.at[3]),
    ]
    for load in loads:
        load.start()

    barrier = pltpu.get_barrier_semaphore()

    @pl.loop(1, NS)
    def _(i):
        pl.semaphore_signal(barrier, inc=1, device_id=((s + i) % NS, y), device_id_type=MESH)

    @pl.loop(0, 3 * 8)
    def _(i):
        k = i % 8
        peer = ((k // 2) * (2 * NZ) + z * 2 + k % 2, (y + 1 + i // 8) % NM)
        pl.semaphore_signal(barrier, inc=1, device_id=peer, device_id_type=MESH)

    X[M : 2 * M] = jnp.zeros((M, BLK * OBS), jnp.float32)
    for load in loads[:3]:
        load.wait()
    for f in range(3):
        for r in range(ROWS):
            for c in range(2):
                S[f, HALO + r, :, c * OBS : (c + 1) * OBS] = st[c, pl.ds(f * ROWS + r, LM, stride=3 * ROWS), :]
    for r in range(ROWS):
        DB[HALO + r] = jnp.broadcast_to(dp[pl.ds(r, 1), :], (8, COLS))
    pl.semaphore_wait(barrier, NS - 1 + 3 * 8)

    left, right = (s + NS - 1) % NS, (s + 1) % NS
    halos = []
    for n, (peer, src, dst) in enumerate(((left, HALO, HALO + ROWS), (right, ROWS, 0))):
        for k, (buf, src_ref, dst_ref) in enumerate(
            (
                (S, S.at[:, pl.ds(src, HALO)], S.at[:, pl.ds(dst, HALO)]),
                (DB, DB.at[pl.ds(src, HALO)], DB.at[pl.ds(dst, HALO)]),
            )
        ):
            halos.append(
                pltpu.make_async_remote_copy(
                    src_ref=src_ref, dst_ref=dst_ref, send_sem=halo_send.at[n, k], recv_sem=halo_recv.at[n, k],
                    device_id=(peer, y), device_id_type=MESH,
                )
            )
            halos[-1].start()
    for halo in halos:
        halo.wait()

    own_v = pltpu.make_async_copy(values.at[0, s], tab_v.at[s], load_sem.at[4])
    own_p = pltpu.make_async_copy(precisions.at[0, s], tab_p.at[s], load_sem.at[5])
    own_v.start()
    own_p.start()

    @pl.loop(1, NS)
    def _(i):
        peer = (s + i) % NS
        for k, (src, tab) in enumerate(((values, tab_v), (precisions, tab_p))):
            pltpu.make_async_remote_copy(
                src_ref=src.at[0, peer], dst_ref=tab.at[s], send_sem=tab_send.at[k], recv_sem=tab_recv.at[k],
                device_id=(peer, y), device_id_type=MESH,
            ).start()

    forecast_heights(s, S, DB, H1, U1, V1, H2)

    @pl.loop(0, ROWS)
    def _(r):
        fc[y, 0, r] = H2[HALO + r]

    def share(src, dst, n, peer):
        return pltpu.make_async_remote_copy(
            src_ref=src, dst_ref=dst, send_sem=ag_send.at[n], recv_sem=ag_recv.at[n],
            device_id=(s, peer), device_id_type=MESH,
        )

    up_h = share(H2.at[pl.ds(HALO, ROWS)], fc.at[y, 0], 0, y_high)
    down_h = share(H2.at[pl.ds(HALO, ROWS)], fc.at[y, 0], 1, y_low)
    up_h.start()
    down_h.start()

    @pl.loop(HALO, HALO + ROWS)
    def _(i):
        u, v, h = U1[i], V1[i], H2[i]
        fc[y, 1, i - HALO] = u - wave_rate * (H2[i + 1] - H2[i - 1]) + turn_rate * v
        fc[y, 2, i - HALO] = v - wave_rate * (east(h) - west(h)) - turn_rate * u

    loads[3].wait()
    loads[4].wait()
    pack_block(y, fc, packed, inverse)
    interpolate([y], packed, inverse, cells, weights, pred)
    up_h.wait()
    down_h.wait()
    half = ROWS // 2
    pass_up = share(fc.at[y_low, 0, pl.ds(0, half)], fc.at[y_low, 0, pl.ds(0, half)], 2, y_high)
    pass_down = share(fc.at[y_high, 0, pl.ds(half, half)], fc.at[y_high, 0, pl.ds(half, half)], 3, y_low)
    pass_up.start()
    pass_down.start()
    up_w = share(fc.at[y, pl.ds(1, 2)], fc.at[y, pl.ds(1, 2)], 4, y_high)
    down_w = share(fc.at[y, pl.ds(1, 2)], fc.at[y, pl.ds(1, 2)], 5, y_low)
    up_w.start()
    down_w.start()
    pack_block(y_low, fc, packed, inverse)
    pack_block(y_high, fc, packed, inverse)
    pass_up.wait()
    pass_down.wait()
    pack_block(y_far, fc, packed, inverse)
    interpolate([y_low, y_high, y_far], packed, inverse, cells, weights, pred)

    own_v.wait()
    own_p.wait()
    for k, tab in enumerate((tab_v, tab_p)):
        everyone = tab.at[pl.ds(0, NS - 1)]
        pltpu.make_async_copy(everyone, everyone, tab_recv.at[k]).wait()
        pltpu.make_async_copy(everyone, everyone, tab_send.at[k]).wait()

    scale = math.sqrt((M - 1) / N_OBS)

    @pl.loop(0, BLK)
    def _(b):
        t = target[y * BLK + b]
        seen = tab_v[t // 2, pl.ds(t % 2, 1), :]
        factor = tab_p[t // 2, pl.ds(t % 2, 1), :] * scale
        parts = [pred[yb, b] for yb in range(NM)]
        middle = jnp.sum(parts[0] + parts[1] + parts[2] + parts[3], axis=0, keepdims=True) * (1.0 / M)
        at = pl.ds(pl.multiple_of(b * OBS, OBS), OBS)
        for yb in range(NM):
            X[yb * LM : (yb + 1) * LM, at] = (parts[yb] - middle) * factor
        X[M : M + 1, at] = (seen - middle) * factor

    gram = lax.dot_general(
        X[0:M], X[...], (((1,), (1,)), ((), ())), precision=HIGHEST, preferred_element_type=jnp.float32
    )
    for q in range(GROUP):
        Gs[q] = gram[2 * q : 2 * q + 2]

    @pl.loop(1, GROUP)
    def _(i):
        q = (place + i) % GROUP
        pltpu.make_async_remote_copy(
            src_ref=Gs.at[q], dst_ref=rs.at[place], send_sem=red_send.at[0], recv_sem=red_recv.at[0],
            device_id=member_of(q), device_id_type=MESH,
        ).start()

    rs[place] = Gs[place]
    others = rs.at[pl.ds(0, GROUP - 1)]
    pltpu.make_async_copy(others, others, red_recv.at[0]).wait()
    mine = rs[0]
    for q in range(1, GROUP):
        mine = mine + rs[q]
    zs[...] = mine
    zb[z] = mine

    @pl.loop(1, NZ)
    def _(i):
        other = (z + i) % NZ
        pltpu.make_async_remote_copy(
            src_ref=zs, dst_ref=zb.at[z], send_sem=red_send.at[1], recv_sem=red_recv.at[1],
            device_id=(x * (2 * NZ) + other * 2 + core, y), device_id_type=MESH,
        ).start()

    others_z = zb.at[pl.ds(0, NZ - 1)]
    pltpu.make_async_copy(others_z, others_z, red_recv.at[1]).wait()
    mine = zb[0]
    for q in range(1, NZ):
        mine = mine + zb[q]
    ga[place] = mine

    @pl.loop(1, GROUP)
    def _(i):
        q = (place + i) % GROUP
        pltpu.make_async_remote_copy(
            src_ref=ga.at[place], dst_ref=ga.at[place], send_sem=red_send.at[2], recv_sem=red_recv.at[2],
            device_id=member_of(q), device_id_type=MESH,
        ).start()

    up_w.wait()
    down_w.wait()
    pass_u = share(fc.at[y_low, 1], fc.at[y_low, 1], 6, y_high)
    pass_v = share(fc.at[y_high, 2], fc.at[y_high, 2], 7, y_low)
    pass_u.start()
    pass_v.start()
    pltpu.make_async_copy(others, others, red_send.at[0]).wait()
    pltpu.make_async_copy(others_z, others_z, red_send.at[1]).wait()
    others_a = ga.at[pl.ds(0, GROUP - 1)]
    pltpu.make_async_copy(others_a, others_a, red_recv.at[2]).wait()
    pltpu.make_async_copy(others_a, others_a, red_send.at[2]).wait()
    for q in range(GROUP):
        total[2 * q : 2 * q + 2] = ga[q]
    pass_u.wait()
    pass_v.wait()


def combine_kernel(total, fc, out, inv_ref, held, sem):
    y = lax.axis_index("mem")
    g = total[...]
    row = lax.broadcasted_iota(jnp.int32, (M, 2 * M), 0)
    lane = lax.broadcasted_iota(jnp.int32, (M, 2 * M), 1)
    proj = g[:, M : M + 1]
    eye = jnp.where(lane == row + M, 1.0, 0.0)
    work = jnp.where(lane < M, g + jnp.where(lane == row, float(M - 1), 0.0), eye)
    for k in range(M - 1):
        pivot = work[k : k + 1, :]
        ratio = work[:, k : k + 1] * (1.0 / work[k : k + 1, k : k + 1])
        work = work - jnp.where(row > k, ratio * pivot, 0.0)
    diagonal = jnp.sum(jnp.where(lane == row, work, 0.0), axis=1, keepdims=True)
    lower_inv = work[:, M:] * (1.0 / jnp.sqrt(diagonal))
    inv_ref[...] = lower_inv
    square = jnp.where(row[:, :M] == lane[:, :M], 1.0, 0.0)
    proj_row = jnp.broadcast_to(jnp.sum(square * proj, axis=0, keepdims=True), (8, M))
    first = lax.dot_general(
        proj_row, lower_inv, (((1,), (1,)), ((), ())), precision=HIGHEST, preferred_element_type=jnp.float32
    )
    mean_weights = jnp.dot(first, lower_inv, precision=HIGHEST, preferred_element_type=jnp.float32)[0:1]
    coef = mean_weights + math.sqrt(M - 1) * inv_ref[pl.ds(pl.multiple_of(y * LM, LM), LM), :]
    mixing = coef + (1.0 - jnp.sum(coef, axis=1, keepdims=True)) * (1.0 / M)
    for f in range(3):

        @pl.loop(0, ROWS)
        def _(r):
            prior = jnp.concatenate([fc[yb, f, r] for yb in range(NM)], axis=0)
            new = jnp.dot(mixing, prior, precision=HIGHEST, preferred_element_type=jnp.float32)
            for c in range(2):
                held[c, pl.ds(f * ROWS + r, LM, stride=3 * ROWS), :] = new[:, c * OBS : (c + 1) * OBS]

    stores = [pltpu.make_async_copy(held.at[c], out.at[:, pl.ds(c * OBS, OBS)], sem.at[c]) for c in range(2)]
    for store in stores:
        store.start()
    for store in stores:
        store.wait()


def local(state, depth, obs_cells, obs_weights, owner_map, obs_values, obs_precision):
    owners = owner_map[:, 0]
    same = (owners[:, None] == owners[None, :]).astype(jnp.int32)
    order = jnp.arange(owners.shape[0], dtype=jnp.int32)
    earlier = (order[:, None] < order[None, :]).astype(jnp.int32)
    target = owners * 2 + jnp.sum(same * earlier, axis=0)
    any_space = pl.BlockSpec(memory_space=pl.ANY)
    f32 = jnp.float32
    fc, total = pl.pallas_call(
        main_kernel,
        name="forecast_and_reduce",
        out_shape=(
            jax.ShapeDtypeStruct((NM, 3, ROWS, LM, COLS), f32),
            jax.ShapeDtypeStruct((M, 2 * M), f32),
        ),
        in_specs=[pl.BlockSpec(memory_space=pltpu.SMEM)] + [any_space] * 6,
        out_specs=(pl.BlockSpec(memory_space=pltpu.VMEM), pl.BlockSpec(memory_space=pltpu.VMEM)),
        scratch_shapes=[
            pltpu.VMEM((2, LM * 3 * ROWS, OBS), f32),
            pltpu.VMEM((ROWS, COLS), f32),
            pltpu.VMEM((4, BLK, OBS), jnp.int32),
            pltpu.VMEM((4, BLK, OBS), f32),
            pltpu.VMEM((3, EXT, LM, COLS), f32),
            pltpu.VMEM((EXT, 8, COLS), f32),
            pltpu.VMEM((EXT, LM, COLS), f32),
            pltpu.VMEM((EXT, LM, COLS), f32),
            pltpu.VMEM((EXT, LM, COLS), f32),
            pltpu.VMEM((EXT, LM, COLS), f32),
            pltpu.VMEM((NM, ROWS, 8, COLS), jnp.int32),
            pltpu.VMEM((NM, LM, OBS), f32),
            pltpu.VMEM((NM, BLK, LM, OBS), f32),
            pltpu.VMEM((2 * M, BLK * OBS), f32),
            pltpu.VMEM((NS, 2, OBS), f32),
            pltpu.VMEM((NS, 2, OBS), f32),
            pltpu.VMEM((GROUP, 2, 2 * M), f32),
            pltpu.VMEM((GROUP, 2, 2 * M), f32),
            pltpu.VMEM((2, 2 * M), f32),
            pltpu.VMEM((NZ, 2, 2 * M), f32),
            pltpu.VMEM((GROUP, 2, 2 * M), f32),
            pltpu.SemaphoreType.DMA((7,)),
            pltpu.SemaphoreType.DMA((2, 2)),
            pltpu.SemaphoreType.DMA((2, 2)),
            pltpu.SemaphoreType.DMA((8,)),
            pltpu.SemaphoreType.DMA((8,)),
            pltpu.SemaphoreType.DMA((2,)),
            pltpu.SemaphoreType.DMA((2,)),
            pltpu.SemaphoreType.DMA((3,)),
            pltpu.SemaphoreType.DMA((3,)),
        ],
        compiler_params=pltpu.CompilerParams(collective_id=0, has_side_effects=True, vmem_limit_bytes=40 << 20),
    )(target, state.reshape(LM * 3 * ROWS, COLS), depth, obs_cells, obs_weights, obs_values, obs_precision)
    vmem = pl.BlockSpec(memory_space=pltpu.VMEM)
    out = pl.pallas_call(
        combine_kernel,
        name="combine_members",
        out_shape=jax.ShapeDtypeStruct((LM * 3 * ROWS, COLS), f32),
        in_specs=[vmem, vmem],
        out_specs=any_space,
        scratch_shapes=[
            pltpu.VMEM((M, M), f32),
            pltpu.VMEM((2, LM * 3 * ROWS, OBS), f32),
            pltpu.SemaphoreType.DMA((2,)),
        ],
        compiler_params=pltpu.CompilerParams(vmem_limit_bytes=40 << 20),
    )(total, fc)
    return out.reshape(LM, 3, ROWS, COLS)


def solution(mesh):
    return jax.shard_map(
        local,
        mesh=mesh,
        in_specs=(
            P("mem", None, "space", None),
            P("space", None),
            P(None, "space", None),
            P(None, "space", None),
            P("space", None),
            P("space", None, None, None),
            P("space", None, None, None),
        ),
        out_specs=P("mem", None, "space", None),
        check_vma=False,
    )
```

```python
import math

import jax
import jax.numpy as jnp
from jax import lax
from jax.experimental import pallas as pl
from jax.experimental.pallas import tpu as pltpu
from jax.sharding import PartitionSpec as P

M = 64
NS = 128
NM = 4
NZ = 16
GROUP = 32
LM = M // NM
ROWS = 16
COLS = 256
HALO = 4
EXT = ROWS + 2 * HALO
BLK = 16
OBS = 128
N_OBS = 8192 * 128
GROUPS = (slice(0, 8), slice(8, 16))
EAST, HEIGHT, NORTH = 0, 1, 2
FIELD = (HEIGHT, EAST, NORTH)
MESH = pl.DeviceIdType.MESH
HIGHEST = lax.Precision.HIGHEST
mass_rate = 0.2
wave_rate = 0.2
turn_rate = 0.1


def east(field):
    return pltpu.roll(field, COLS - 1, 1)


def west(field):
    return pltpu.roll(field, 1, 1)


def height_step(i, keep, S, DB, H1):
    for g in GROUPS:
        flux = DB[i] * S[NORTH, i, g]
        change = DB[i + 1] * S[EAST, i + 1, g] - DB[i - 1] * S[EAST, i - 1, g] + (east(flux) - west(flux))
        H1[i, g] = (S[HEIGHT, i, g] - mass_rate * change) * keep


def wind_step(i, S, H1, U1, V1):
    for g in GROUPS:
        u, v, h = S[EAST, i, g], S[NORTH, i, g], H1[i, g]
        U1[i, g] = u - wave_rate * (H1[i + 1, g] - H1[i - 1, g]) + turn_rate * v
        V1[i, g] = v - wave_rate * (east(h) - west(h)) - turn_rate * u


def second_height(i, keep, DB, H1, U1, V1, H2):
    for g in GROUPS:
        flux = DB[i] * V1[i, g]
        change = DB[i + 1] * U1[i + 1, g] - DB[i - 1] * U1[i - 1, g] + (east(flux) - west(flux))
        H2[i, g] = (H1[i, g] - mass_rate * change) * keep


def pack_block(yb, fc, packed, inverse):
    top = lax.fori_loop(
        0, ROWS, lambda r, t: jnp.maximum(t, jnp.abs(fc[yb, 0, r])), jnp.zeros((LM, COLS), jnp.float32)
    )
    top = jnp.maximum(jnp.max(top, axis=1, keepdims=True), 1e-30)
    scale = 32000.0 / top
    inverse[yb] = jnp.broadcast_to(top * (1.0 / 32000.0), (LM, OBS))

    @pl.loop(0, ROWS)
    def _(r):
        q = jnp.floor(fc[yb, 0, r] * scale + 0.5).astype(jnp.int32)
        packed[yb, r] = (q[0:8] << 16) | (q[8:16] & 0xFFFF)


def interpolate(blocks, packed, inverse, cells, weights, pred):
    for half in range(2):

        @pl.loop(0, BLK)
        def _(b):
            lane, chunk, weight = [], [], []
            for k in range(2):
                cell = jnp.broadcast_to(cells[half * 2 + k, pl.ds(b, 1), :], (8, OBS))
                lane.append(cell & (OBS - 1))
                chunk.append(cell >> 7)
                weight.append(jnp.broadcast_to(weights[half * 2 + k, pl.ds(b, 1), :], (8, OBS)))
            held = [[jnp.zeros((8, OBS), jnp.int32) for _ in blocks] for _ in range(2)]
            for c in range(ROWS * COLS // OBS):
                row, col = c // 2, (c % 2) * OBS
                here = [chunk[k] == c for k in range(2)]
                for g, yb in enumerate(blocks):
                    values = packed[yb, row, :, col : col + OBS]
                    for k in range(2):
                        found = jnp.take_along_axis(values, lane[k], axis=1, mode="promise_in_bounds")
                        held[k][g] = jnp.where(here[k], found, held[k][g])
            for g, yb in enumerate(blocks):
                high = sum((held[k][g] >> 16).astype(jnp.float32) * weight[k] for k in range(2))
                low = sum(((held[k][g] << 16) >> 16).astype(jnp.float32) * weight[k] for k in range(2))
                part = jnp.concatenate([high, low], axis=0) * inverse[yb]
                pred[yb, b] = part if half == 0 else pred[yb, b] + part


def main_kernel(
    owners_hbm, state, depth, cells_hbm, weights_hbm, values, precisions, fc, total,
    owners, target, st, dp, cells, weights, S, DB, H1, U1, V1, H2, packed, inverse, pred, X, tab_v, tab_p, Gs, rs, zs, zb, ga,
    load_sem, halo_send, halo_recv, ag_send, ag_recv, tab_send, tab_recv, red_send, red_recv, round_sem,
):
    s = lax.axis_index("space")
    y = lax.axis_index("mem")
    core = s % 2
    z = (s // 2) % NZ
    x = s // (2 * NZ)
    y_low, y_high, y_far = (y + 3) % NM, (y + 1) % NM, (y + 2) % NM
    place = (x * NM + y) * 2 + core
    left, right = (s + NS - 1) % NS, (s + 1) % NS

    def member_of(q):
        return ((q // 8) * (2 * NZ) + z * 2 + q % 2, (q // 2) % NM)

    def along_z(step):
        return (x * (2 * NZ) + ((z + step + NZ) % NZ) * 2 + core, y)

    def along_x(step):
        return (((x + step + 4) % 4) * (2 * NZ) + z * 2 + core, y)

    def along_y(step):
        return (s, (y + step + NM) % NM)

    partner = (s + 1 - 2 * core, y)
    own_rows = pl.ds(pl.multiple_of(y * BLK, BLK), BLK)
    loads = [
        pltpu.make_async_copy(state.at[:, pl.ds(0, OBS)], st.at[0], load_sem.at[0]),
        pltpu.make_async_copy(state.at[:, pl.ds(OBS, OBS)], st.at[1], load_sem.at[1]),
        pltpu.make_async_copy(depth, dp, load_sem.at[2]),
        pltpu.make_async_copy(cells_hbm.at[:, own_rows], cells, load_sem.at[3]),
        pltpu.make_async_copy(weights_hbm.at[:, own_rows], weights, load_sem.at[4]),
        pltpu.make_async_copy(owners_hbm, owners, load_sem.at[5]),
    ]
    for load in loads:
        load.start()

    barrier = pltpu.get_barrier_semaphore()
    cross = (left + core * (right - left), y)
    near = [partner, cross, along_z(1), along_z(-1), along_x(1), along_x(-1), along_y(1), along_y(-1)]
    for peer in near:
        pl.semaphore_signal(barrier, inc=1, device_id=peer, device_id_type=MESH)

    rounds = [
        (along_z(1), along_z(-1)),
        (along_z(2), along_z(-2)),
        (along_z(4), along_z(-4)),
        (partner,),
        (along_x(1), along_x(-1)),
        (along_x(1), along_x(-1)),
        (along_y(1), along_y(-1)),
        (along_y(1), along_y(-1)),
    ]

    def tell(n):
        for peer in rounds[n]:
            pl.semaphore_signal(round_sem.at[n], inc=1, device_id=peer, device_id_type=MESH)

    def hear(n):
        pl.semaphore_wait(round_sem.at[n], len(rounds[n]))

    for load in loads[:3]:
        load.wait()
    for f in range(3):
        for r in range(ROWS):
            for c in range(2):
                S[FIELD[f], HALO + r, :, c * OBS : (c + 1) * OBS] = st[c, pl.ds(f * ROWS + r, LM, stride=3 * ROWS), :]
    for r in range(ROWS):
        DB[HALO + r] = jnp.broadcast_to(dp[pl.ds(r, 1), :], (8, COLS))
    pl.semaphore_wait(barrier, len(near))

    halos = []
    for n, (peer, src, dst) in enumerate(((left, HALO, HALO + ROWS), (right, ROWS, 0))):
        for k, (buf, lead, skip, rows) in enumerate(
            ((S, (EAST,), 0, HALO), (S, (pl.ds(HEIGHT, 2),), n, HALO - 1), (DB, (), 0, HALO))
        ):
            halos.append(
                pltpu.make_async_remote_copy(
                    src_ref=buf.at[(*lead, pl.ds(src + skip, rows))], dst_ref=buf.at[(*lead, pl.ds(dst + skip, rows))],
                    send_sem=halo_send.at[n, k], recv_sem=halo_recv.at[n, k], device_id=(peer, y), device_id_type=MESH,
                )
            )
            halos[-1].start()

    tell(0)

    @pl.loop(HALO + 1, HALO + ROWS - 1, unroll=2)
    def _(i):
        height_step(i, 1.0, S, DB, H1)

    hear(0)
    tell(1)

    @pl.loop(HALO + 2, HALO + ROWS - 2, unroll=2)
    def _(i):
        wind_step(i, S, H1, U1, V1)

    hear(1)
    tell(2)

    @pl.loop(HALO + 3, HALO + ROWS - 3, unroll=2)
    def _(i):
        second_height(i, 1.0, DB, H1, U1, V1, H2)

    hear(2)
    tell(3)
    for halo in halos:
        halo.wait()

    inside_low = jnp.where(s > 0, 1.0, 0.0).astype(jnp.float32)
    inside_high = jnp.where(s < NS - 1, 1.0, 0.0).astype(jnp.float32)
    for i in range(HALO):
        DB[i] = DB[i] * inside_low
        DB[HALO + ROWS + i] = DB[HALO + ROWS + i] * inside_high
    for i in range(1, 5):
        height_step(i, inside_low if i < HALO else 1.0, S, DB, H1)
        height_step(EXT - 1 - i, inside_high if i < HALO else 1.0, S, DB, H1)
    hear(3)
    tell(4)
    for i in range(2, 6):
        wind_step(i, S, H1, U1, V1)
        wind_step(EXT - 1 - i, S, H1, U1, V1)
    hear(4)
    tell(5)
    for i in range(3, 7):
        second_height(i, inside_low if i < HALO else 1.0, DB, H1, U1, V1, H2)
        second_height(EXT - 1 - i, inside_high if i < HALO else 1.0, DB, H1, U1, V1, H2)

    def share(src, dst, n, peer):
        copy = pltpu.make_async_remote_copy(
            src_ref=src, dst_ref=dst, send_sem=ag_send.at[n], recv_sem=ag_recv.at[n],
            device_id=(s, peer), device_id_type=MESH,
        )
        copy.start()
        return copy

    half = ROWS // 2
    first, last = pl.ds(0, half), pl.ds(half, half)
    sent_first, sent_last = H2.at[pl.ds(HALO, half)], H2.at[pl.ds(HALO + half, half)]
    up_first = share(sent_first, fc.at[y, 0, first], 0, y_high)
    down_first = share(sent_last, fc.at[y, 0, last], 1, y_low)
    up_last = share(sent_last, fc.at[y, 0, last], 2, y_high)
    down_last = share(sent_first, fc.at[y, 0, first], 3, y_low)

    @pl.loop(0, ROWS, unroll=2)
    def _(r):
        fc[y, 0, r] = H2[HALO + r]

    hear(5)
    tell(6)
    own_v = pltpu.make_async_copy(values.at[0, s], tab_v.at[s], load_sem.at[6])
    own_p = pltpu.make_async_copy(precisions.at[0, s], tab_p.at[s], load_sem.at[7])
    own_v.start()
    own_p.start()

    @pl.loop(1, NS)
    def _(i):
        peer = (s + i) % NS
        for k, (src, tab) in enumerate(((values, tab_v), (precisions, tab_p))):
            pltpu.make_async_remote_copy(
                src_ref=src.at[0, peer], dst_ref=tab.at[s], send_sem=tab_send.at[k], recv_sem=tab_recv.at[k],
                device_id=(peer, y), device_id_type=MESH,
            ).start()

    loads[3].wait()
    loads[4].wait()
    loads[5].wait()
    pack_block(y, fc, packed, inverse)
    interpolate([y], packed, inverse, cells, weights, pred)
    hear(6)
    tell(7)
    up_first.wait_recv()
    down_first.wait_recv()
    pass_up = share(fc.at[y_low, 0, first], fc.at[y_low, 0, first], 4, y_high)
    pass_down = share(fc.at[y_high, 0, last], fc.at[y_high, 0, last], 5, y_low)

    @pl.loop(HALO, HALO + ROWS, unroll=2)
    def _(i):
        u, v, h = U1[i], V1[i], H2[i]
        fc[y, 1, i - HALO] = u - wave_rate * (H2[i + 1] - H2[i - 1]) + turn_rate * v
        fc[y, 2, i - HALO] = v - wave_rate * (east(h) - west(h)) - turn_rate * u

    up_w = share(fc.at[y, pl.ds(1, 2)], fc.at[y, pl.ds(1, 2)], 6, y_high)
    down_w = share(fc.at[y, pl.ds(1, 2)], fc.at[y, pl.ds(1, 2)], 7, y_low)

    @pl.loop(0, BLK)
    def _(b):
        me = y * BLK + b
        owner = owners[me]
        slot = jnp.int32(0)
        for other in range(8192 // NS):
            slot = slot + jnp.where((owners[other] == owner) & (other < me), 1, 0)
        target[b] = owner * 2 + slot

    up_last.wait_recv()
    down_last.wait_recv()
    pack_block(y_low, fc, packed, inverse)
    pack_block(y_high, fc, packed, inverse)
    pass_up.wait_recv()
    pass_down.wait_recv()
    pack_block(y_far, fc, packed, inverse)
    interpolate([y_low, y_high, y_far], packed, inverse, cells, weights, pred)
    up_w.wait_recv()
    down_w.wait_recv()
    pass_u = share(fc.at[y_low, 1], fc.at[y_low, 1], 8, y_high)
    pass_v = share(fc.at[y_high, 2], fc.at[y_high, 2], 9, y_low)
    hear(7)

    own_v.wait()
    own_p.wait()
    for k, tab in enumerate((tab_v, tab_p)):
        everyone = tab.at[pl.ds(0, NS - 1)]
        pltpu.make_async_copy(everyone, everyone, tab_recv.at[k]).wait()

    scale = math.sqrt((M - 1) / N_OBS)
    X[M : 2 * M] = jnp.zeros((M, BLK * OBS), jnp.float32)

    @pl.loop(0, BLK)
    def _(b):
        t = target[b]
        seen = tab_v[t // 2, pl.ds(t % 2, 1), :]
        factor = tab_p[t // 2, pl.ds(t % 2, 1), :] * scale
        parts = [pred[yb, b] for yb in range(NM)]
        middle = jnp.sum(parts[0] + parts[1] + parts[2] + parts[3], axis=0, keepdims=True) * (1.0 / M)
        at = pl.ds(pl.multiple_of(b * OBS, OBS), OBS)
        for yb in range(NM):
            X[yb * LM : (yb + 1) * LM, at] = (parts[yb] - middle) * factor
        X[M : M + 1, at] = (seen - middle) * factor

    gram = lax.dot_general(
        X[0:M], X[...], (((1,), (1,)), ((), ())), precision=HIGHEST, preferred_element_type=jnp.float32
    )
    for q in range(GROUP):
        Gs[q] = gram[2 * q : 2 * q + 2]

    @pl.loop(1, GROUP)
    def _(i):
        q = (place + i) % GROUP
        pltpu.make_async_remote_copy(
            src_ref=Gs.at[q], dst_ref=rs.at[place], send_sem=red_send.at[0], recv_sem=red_recv.at[0],
            device_id=member_of(q), device_id_type=MESH,
        ).start()

    rs[place] = Gs[place]
    others = rs.at[pl.ds(0, GROUP - 1)]
    pltpu.make_async_copy(others, others, red_recv.at[0]).wait()
    mine = rs[0]
    for q in range(1, GROUP):
        mine = mine + rs[q]
    zs[...] = mine
    zb[z] = mine

    @pl.loop(1, NZ)
    def _(i):
        other = (z + i) % NZ
        pltpu.make_async_remote_copy(
            src_ref=zs, dst_ref=zb.at[z], send_sem=red_send.at[1], recv_sem=red_recv.at[1],
            device_id=(x * (2 * NZ) + other * 2 + core, y), device_id_type=MESH,
        ).start()

    others_z = zb.at[pl.ds(0, NZ - 1)]
    pltpu.make_async_copy(others_z, others_z, red_recv.at[1]).wait()
    mine = zb[0]
    for q in range(1, NZ):
        mine = mine + zb[q]
    ga[place] = mine

    @pl.loop(1, GROUP)
    def _(i):
        q = (place + i) % GROUP
        pltpu.make_async_remote_copy(
            src_ref=ga.at[place], dst_ref=ga.at[place], send_sem=red_send.at[2], recv_sem=red_recv.at[2],
            device_id=member_of(q), device_id_type=MESH,
        ).start()

    pltpu.make_async_copy(others, others, red_send.at[0]).wait()
    pltpu.make_async_copy(others_z, others_z, red_send.at[1]).wait()
    others_a = ga.at[pl.ds(0, GROUP - 1)]
    pltpu.make_async_copy(others_a, others_a, red_recv.at[2]).wait()
    pltpu.make_async_copy(others_a, others_a, red_send.at[2]).wait()
    for q in range(GROUP):
        total[2 * q : 2 * q + 2] = ga[q]
    pass_u.wait_recv()
    pass_v.wait_recv()
    for copy in (up_first, down_first, up_last, down_last, pass_up, pass_down, up_w, down_w, pass_u, pass_v):
        copy.wait_send()
    for k, tab in enumerate((tab_v, tab_p)):
        everyone = tab.at[pl.ds(0, NS - 1)]
        pltpu.make_async_copy(everyone, everyone, tab_send.at[k]).wait()


def combine_kernel(total, fc, out, inv_ref, held, sem):
    y = lax.axis_index("mem")
    g = total[...]
    row = lax.broadcasted_iota(jnp.int32, (M, 2 * M), 0)
    lane = lax.broadcasted_iota(jnp.int32, (M, 2 * M), 1)
    proj = g[:, M : M + 1]
    eye = jnp.where(lane == row + M, 1.0, 0.0)
    work = jnp.where(lane < M, g + jnp.where(lane == row, float(M - 1), 0.0), eye)
    for k in range(M - 1):
        pivot = work[k : k + 1, :]
        ratio = work[:, k : k + 1] * (1.0 / work[k : k + 1, k : k + 1])
        work = work - jnp.where(row > k, ratio * pivot, 0.0)
    diagonal = jnp.sum(jnp.where(lane == row, work, 0.0), axis=1, keepdims=True)
    lower_inv = work[:, M:] * (1.0 / jnp.sqrt(diagonal))
    inv_ref[...] = lower_inv
    square = jnp.where(row[:, :M] == lane[:, :M], 1.0, 0.0)
    proj_row = jnp.broadcast_to(jnp.sum(square * proj, axis=0, keepdims=True), (8, M))
    first = lax.dot_general(
        proj_row, lower_inv, (((1,), (1,)), ((), ())), precision=HIGHEST, preferred_element_type=jnp.float32
    )
    mean_weights = jnp.dot(first, lower_inv, precision=HIGHEST, preferred_element_type=jnp.float32)[0:1]
    coef = mean_weights + math.sqrt(M - 1) * inv_ref[pl.ds(pl.multiple_of(y * LM, LM), LM), :]
    mixing = coef + (1.0 - jnp.sum(coef, axis=1, keepdims=True)) * (1.0 / M)
    for f in range(3):

        @pl.loop(0, ROWS)
        def _(r):
            prior = jnp.concatenate([fc[yb, f, r] for yb in range(NM)], axis=0)
            new = jnp.dot(mixing, prior, precision=HIGHEST, preferred_element_type=jnp.float32)
            for c in range(2):
                held[c, pl.ds(f * ROWS + r, LM, stride=3 * ROWS), :] = new[:, c * OBS : (c + 1) * OBS]

    stores = [pltpu.make_async_copy(held.at[c], out.at[:, pl.ds(c * OBS, OBS)], sem.at[c]) for c in range(2)]
    for store in stores:
        store.start()
    for store in stores:
        store.wait()


def local(state, depth, obs_cells, obs_weights, owner_map, obs_values, obs_precision):
    any_space = pl.BlockSpec(memory_space=pltpu.HBM)
    f32 = jnp.float32
    fc, total = pl.pallas_call(
        main_kernel,
        name="forecast_and_reduce",
        out_shape=(
            jax.ShapeDtypeStruct((NM, 3, ROWS, LM, COLS), f32),
            jax.ShapeDtypeStruct((M, 2 * M), f32),
        ),
        in_specs=[any_space] * 7,
        out_specs=(pl.BlockSpec(memory_space=pltpu.VMEM), pl.BlockSpec(memory_space=pltpu.VMEM)),
        scratch_shapes=[
            pltpu.SMEM((8192 // NS,), jnp.int32),
            pltpu.SMEM((BLK,), jnp.int32),
            pltpu.VMEM((2, LM * 3 * ROWS, OBS), f32),
            pltpu.VMEM((ROWS, COLS), f32),
            pltpu.VMEM((4, BLK, OBS), jnp.int32),
            pltpu.VMEM((4, BLK, OBS), f32),
            pltpu.VMEM((3, EXT, LM, COLS), f32),
            pltpu.VMEM((EXT, 8, COLS), f32),
            pltpu.VMEM((EXT, LM, COLS), f32),
            pltpu.VMEM((EXT, LM, COLS), f32),
            pltpu.VMEM((EXT, LM, COLS), f32),
            pltpu.VMEM((EXT, LM, COLS), f32),
            pltpu.VMEM((NM, ROWS, 8, COLS), jnp.int32),
            pltpu.VMEM((NM, LM, OBS), f32),
            pltpu.VMEM((NM, BLK, LM, OBS), f32),
            pltpu.VMEM((2 * M, BLK * OBS), f32),
            pltpu.VMEM((NS, 2, OBS), f32),
            pltpu.VMEM((NS, 2, OBS), f32),
            pltpu.VMEM((GROUP, 2, 2 * M), f32),
            pltpu.VMEM((GROUP, 2, 2 * M), f32),
            pltpu.VMEM((2, 2 * M), f32),
            pltpu.VMEM((NZ, 2, 2 * M), f32),
            pltpu.VMEM((GROUP, 2, 2 * M), f32),
            pltpu.SemaphoreType.DMA((8,)),
            pltpu.SemaphoreType.DMA((2, 3)),
            pltpu.SemaphoreType.DMA((2, 3)),
            pltpu.SemaphoreType.DMA((10,)),
            pltpu.SemaphoreType.DMA((10,)),
            pltpu.SemaphoreType.DMA((2,)),
            pltpu.SemaphoreType.DMA((2,)),
            pltpu.SemaphoreType.DMA((3,)),
            pltpu.SemaphoreType.DMA((3,)),
            pltpu.SemaphoreType.REGULAR((8,)),
        ],
        compiler_params=pltpu.CompilerParams(collective_id=0, has_side_effects=True, vmem_limit_bytes=40 << 20),
    )(
        *(
            pltpu.with_memory_space_constraint(a, pltpu.HBM)
            for a in (
                owner_map.reshape(-1), state.reshape(LM * 3 * ROWS, COLS), depth,
                obs_cells, obs_weights, obs_values, obs_precision,
            )
        )
    )
    vmem = pl.BlockSpec(memory_space=pltpu.VMEM)
    out = pl.pallas_call(
        combine_kernel,
        name="combine_members",
        out_shape=jax.ShapeDtypeStruct((LM * 3 * ROWS, COLS), f32),
        in_specs=[vmem, vmem],
        out_specs=any_space,
        scratch_shapes=[
            pltpu.VMEM((M, M), f32),
            pltpu.VMEM((2, LM * 3 * ROWS, OBS), f32),
            pltpu.SemaphoreType.DMA((2,)),
        ],
        compiler_params=pltpu.CompilerParams(vmem_limit_bytes=40 << 20),
    )(total, fc)
    return out.reshape(LM, 3, ROWS, COLS)


def solution(mesh):
    return jax.shard_map(
        local,
        mesh=mesh,
        in_specs=(
            P("mem", None, "space", None),
            P("space", None),
            P(None, "space", None),
            P(None, "space", None),
            P("space", None),
            P("space", None, None, None),
            P("space", None, None, None),
        ),
        out_specs=P("mem", None, "space", None),
        check_vma=False,
    )
```

```python
import math

import jax
import jax.numpy as jnp
from jax import lax
from jax.experimental import pallas as pl
from jax.experimental.pallas import tpu as pltpu
from jax.sharding import PartitionSpec as P

M = 64
NS = 128
NM = 4
NZ = 16
GROUP = 32
LM = M // NM
ROWS = 16
COLS = 256
HALO = 4
EXT = ROWS + 2 * HALO
BLK = 16
OBS = 128
N_OBS = 8192 * 128
GROUPS = (slice(0, 8), slice(8, 16))
EAST, HEIGHT, NORTH = 0, 1, 2
FIELD = (HEIGHT, EAST, NORTH)
MESH = pl.DeviceIdType.MESH
HIGHEST = lax.Precision.HIGHEST
mass_rate = 0.2
wave_rate = 0.2
turn_rate = 0.1


def east(field):
    return pltpu.roll(field, COLS - 1, 1)


def west(field):
    return pltpu.roll(field, 1, 1)


def height_step(i, keep, S, DB, H1):
    for g in GROUPS:
        flux = DB[i] * S[NORTH, i, g]
        change = DB[i + 1] * S[EAST, i + 1, g] - DB[i - 1] * S[EAST, i - 1, g] + (east(flux) - west(flux))
        H1[i, g] = (S[HEIGHT, i, g] - mass_rate * change) * keep


def wind_step(i, S, H1, U1, V1):
    for g in GROUPS:
        u, v, h = S[EAST, i, g], S[NORTH, i, g], H1[i, g]
        U1[i, g] = u - wave_rate * (H1[i + 1, g] - H1[i - 1, g]) + turn_rate * v
        V1[i, g] = v - wave_rate * (east(h) - west(h)) - turn_rate * u


def second_height(i, keep, DB, H1, U1, V1, H2):
    for g in GROUPS:
        flux = DB[i] * V1[i, g]
        change = DB[i + 1] * U1[i + 1, g] - DB[i - 1] * U1[i - 1, g] + (east(flux) - west(flux))
        H2[i, g] = (H1[i, g] - mass_rate * change) * keep


def pack_block(yb, fc, packed, inverse):
    top = lax.fori_loop(
        0, ROWS, lambda r, t: jnp.maximum(t, jnp.abs(fc[yb, 0, r])), jnp.zeros((LM, COLS), jnp.float32)
    )
    top = jnp.maximum(jnp.max(top, axis=1, keepdims=True), 1e-30)
    scale = 32000.0 / top
    inverse[yb] = jnp.broadcast_to(top * (1.0 / 32000.0), (LM, OBS))

    @pl.loop(0, ROWS)
    def _(r):
        q = jnp.floor(fc[yb, 0, r] * scale + 0.5).astype(jnp.int32)
        packed[yb, r] = (q[0:8] << 16) | (q[8:16] & 0xFFFF)


def interpolate(halves, blocks, packed, inverse, cells, weights, pred):
    for half in halves:

        @pl.loop(0, BLK)
        def _(b):
            lane, chunk, weight = [], [], []
            for k in range(2):
                cell = jnp.broadcast_to(cells[half * 2 + k, pl.ds(b, 1), :], (8, OBS))
                lane.append(cell & (OBS - 1))
                chunk.append(cell >> 7)
                weight.append(jnp.broadcast_to(weights[half * 2 + k, pl.ds(b, 1), :], (8, OBS)))
            held = [[jnp.zeros((8, OBS), jnp.int32) for _ in blocks] for _ in range(2)]
            for c in range(ROWS * COLS // OBS):
                row, col = c // 2, (c % 2) * OBS
                here = [chunk[k] == c for k in range(2)]
                for g, yb in enumerate(blocks):
                    values = packed[yb, row, :, col : col + OBS]
                    for k in range(2):
                        found = jnp.take_along_axis(values, lane[k], axis=1, mode="promise_in_bounds")
                        held[k][g] = jnp.where(here[k], found, held[k][g])
            for g, yb in enumerate(blocks):
                high = sum((held[k][g] >> 16).astype(jnp.float32) * weight[k] for k in range(2))
                low = sum(((held[k][g] << 16) >> 16).astype(jnp.float32) * weight[k] for k in range(2))
                part = jnp.concatenate([high, low], axis=0) * inverse[yb]
                pred[yb, b] = part if half == 0 else pred[yb, b] + part


def tree_sum(terms):
    while len(terms) > 1:
        terms = [sum(terms[i : i + 2][1:], terms[i]) for i in range(0, len(terms), 2)]
    return terms[0]


def main_kernel(
    owners_hbm, state, depth, cells_hbm, weights_hbm, values, precisions, fc, total,
    owners, target, st, dp, cells, weights, S, DB, H1, U1, V1, H2, packed, inverse, pred, X, sent, tab, Gs, rs, zs, zb, ga,
    load_sem, halo_send, halo_recv, ag_send, ag_recv, tab_send, tab_recv, red_send, red_recv, round_sem,
):
    s = lax.axis_index("space")
    y = lax.axis_index("mem")
    core = s % 2
    z = (s // 2) % NZ
    x = s // (2 * NZ)
    y_low, y_high, y_far = (y + 3) % NM, (y + 1) % NM, (y + 2) % NM
    place = (x * NM + y) * 2 + core
    left, right = (s + NS - 1) % NS, (s + 1) % NS

    def along_z(step):
        return (x * (2 * NZ) + ((z + step + NZ) % NZ) * 2 + core, y)

    def along_x(step):
        return (((x + step + 4) % 4) * (2 * NZ) + z * 2 + core, y)

    def along_y(step):
        return (s, (y + step + NM) % NM)

    partner = (s + 1 - 2 * core, y)

    def beside(dx, dy, dc):
        nx, ny, nc = (x + dx) % 4, (y + dy) % NM, core + dc - 2 * dc * core
        return (nx * NM + ny) * 2 + nc, (nx * (2 * NZ) + z * 2 + nc, ny)

    def hops(k, size):
        return min(k, size - k)

    steps = sorted(
        ((dx, dy, dc) for dx in range(4) for dy in range(NM) for dc in range(2) if (dx, dy, dc) != (0, 0, 0)),
        key=lambda d: -(hops(d[0], 4) + hops(d[1], NM)),
    )
    members = [beside(*step) for step in steps]
    ring = [along_z(k) for k in sorted(range(1, NZ), key=lambda k: -hops(k, NZ))]
    own_rows = pl.ds(pl.multiple_of(y * BLK, BLK), BLK)
    loads = [
        pltpu.make_async_copy(state.at[:, pl.ds(0, OBS)], st.at[0], load_sem.at[0]),
        pltpu.make_async_copy(state.at[:, pl.ds(OBS, OBS)], st.at[1], load_sem.at[1]),
        pltpu.make_async_copy(depth, dp, load_sem.at[2]),
        pltpu.make_async_copy(cells_hbm.at[:, own_rows], cells, load_sem.at[3]),
        pltpu.make_async_copy(weights_hbm.at[:, own_rows], weights, load_sem.at[4]),
        pltpu.make_async_copy(owners_hbm, owners, load_sem.at[5]),
        pltpu.make_async_copy(values.at[0], sent.at[:, 0], load_sem.at[6]),
        pltpu.make_async_copy(precisions.at[0], sent.at[:, 1], load_sem.at[7]),
    ]
    for load in loads:
        load.start()

    barrier = pltpu.get_barrier_semaphore()
    cross = (left + core * (right - left), y)
    near = [partner, cross, along_z(1), along_z(-1), along_x(1), along_x(-1), along_y(1), along_y(-1)]
    for peer in near:
        pl.semaphore_signal(barrier, inc=1, device_id=peer, device_id_type=MESH)

    rounds = [
        (along_z(1), along_z(-1)),
        (along_z(2), along_z(-2)),
        (along_z(4), along_z(-4)),
        (partner,),
        (along_x(1), along_x(-1)),
        (along_x(1), along_x(-1)),
        (along_y(1), along_y(-1)),
        (along_y(1), along_y(-1)),
    ]

    def tell(n):
        for peer in rounds[n]:
            pl.semaphore_signal(round_sem.at[n], inc=1, device_id=peer, device_id_type=MESH)

    def hear(n):
        pl.semaphore_wait(round_sem.at[n], len(rounds[n]))

    X[M : 2 * M] = jnp.zeros((M, BLK * OBS), jnp.float32)
    for load in loads[:3]:
        load.wait()
    for f in range(3):
        for r in range(ROWS):
            for c in range(2):
                S[FIELD[f], HALO + r, :, c * OBS : (c + 1) * OBS] = st[c, pl.ds(f * ROWS + r, LM, stride=3 * ROWS), :]
    for r in range(ROWS):
        DB[HALO + r] = jnp.broadcast_to(dp[pl.ds(r, 1), :], (8, COLS))
    pl.semaphore_wait(barrier, len(near))

    halos = []
    for n, (peer, src, dst) in enumerate(((left, HALO, HALO + ROWS), (right, ROWS, 0))):
        for k, (buf, lead, skip, rows) in enumerate(
            ((S, (EAST,), 0, HALO), (S, (pl.ds(HEIGHT, 2),), n, HALO - 1), (DB, (), 0, HALO))
        ):
            halos.append(
                pltpu.make_async_remote_copy(
                    src_ref=buf.at[(*lead, pl.ds(src + skip, rows))], dst_ref=buf.at[(*lead, pl.ds(dst + skip, rows))],
                    send_sem=halo_send.at[n, k], recv_sem=halo_recv.at[n, k], device_id=(peer, y), device_id_type=MESH,
                )
            )
            halos[-1].start()

    tell(0)

    @pl.loop(HALO + 1, HALO + ROWS - 1, unroll=2)
    def _(i):
        height_step(i, 1.0, S, DB, H1)

    hear(0)
    tell(1)

    @pl.loop(HALO + 2, HALO + ROWS - 2, unroll=2)
    def _(i):
        wind_step(i, S, H1, U1, V1)

    hear(1)
    tell(2)

    loads[5].wait()

    @pl.loop(HALO + 3, HALO + ROWS - 3, unroll=2)
    def _(i):
        second_height(i, 1.0, DB, H1, U1, V1, H2)

    @pl.loop(0, BLK)
    def _(b):
        me = y * BLK + b
        owner = owners[me]
        slot = jnp.int32(0)
        for other in range(8192 // NS):
            slot = slot + jnp.where((owners[other] == owner) & (other < me), 1, 0)
        target[b] = owner * 2 + slot

    hear(2)
    tell(3)
    for halo in halos:
        halo.wait()

    inside_low = jnp.where(s > 0, 1.0, 0.0).astype(jnp.float32)
    inside_high = jnp.where(s < NS - 1, 1.0, 0.0).astype(jnp.float32)
    for i in range(HALO):
        DB[i] = DB[i] * inside_low
        DB[HALO + ROWS + i] = DB[HALO + ROWS + i] * inside_high
    for i in range(1, 5):
        height_step(i, inside_low if i < HALO else 1.0, S, DB, H1)
        height_step(EXT - 1 - i, inside_high if i < HALO else 1.0, S, DB, H1)
    hear(3)
    tell(4)
    for i in range(2, 6):
        wind_step(i, S, H1, U1, V1)
        wind_step(EXT - 1 - i, S, H1, U1, V1)
    hear(4)
    tell(5)
    for i in range(3, 7):
        second_height(i, inside_low if i < HALO else 1.0, DB, H1, U1, V1, H2)
        second_height(EXT - 1 - i, inside_high if i < HALO else 1.0, DB, H1, U1, V1, H2)

    def share(src, dst, n, peer):
        copy = pltpu.make_async_remote_copy(
            src_ref=src, dst_ref=dst, send_sem=ag_send.at[n], recv_sem=ag_recv.at[n],
            device_id=(s, peer), device_id_type=MESH,
        )
        copy.start()
        return copy

    half = ROWS // 2
    first, last = pl.ds(0, half), pl.ds(half, half)
    sent_first, sent_last = H2.at[pl.ds(HALO, half)], H2.at[pl.ds(HALO + half, half)]
    up_first = share(sent_first, fc.at[y, 0, first], 0, y_high)
    down_first = share(sent_last, fc.at[y, 0, last], 1, y_low)
    up_last = share(sent_last, fc.at[y, 0, last], 2, y_high)
    down_last = share(sent_first, fc.at[y, 0, first], 3, y_low)

    @pl.loop(0, ROWS, unroll=2)
    def _(r):
        fc[y, 0, r] = H2[HALO + r]

    hear(5)
    tell(6)
    loads[6].wait()
    loads[7].wait()
    tab[s] = sent[s]

    @pl.loop(1, NS)
    def _(i):
        peer = s + i
        peer = peer - jnp.where(peer >= NS, NS, 0)
        pltpu.make_async_remote_copy(
            src_ref=sent.at[peer], dst_ref=tab.at[s], send_sem=tab_send, recv_sem=tab_recv,
            device_id=(peer, y), device_id_type=MESH,
        ).start()

    loads[3].wait()
    loads[4].wait()
    pack_block(y, fc, packed, inverse)
    interpolate([0], [y], packed, inverse, cells, weights, pred)
    hear(6)
    tell(7)
    up_first.wait_recv()
    down_first.wait_recv()
    pass_up = share(fc.at[y_low, 0, first], fc.at[y_low, 0, first], 4, y_high)
    pass_down = share(fc.at[y_high, 0, last], fc.at[y_high, 0, last], 5, y_low)

    @pl.loop(HALO, HALO + ROWS, unroll=2)
    def _(i):
        u, v, h = U1[i], V1[i], H2[i]
        fc[y, 1, i - HALO] = u - wave_rate * (H2[i + 1] - H2[i - 1]) + turn_rate * v
        fc[y, 2, i - HALO] = v - wave_rate * (east(h) - west(h)) - turn_rate * u

    up_w = share(fc.at[y, pl.ds(1, 2)], fc.at[y, pl.ds(1, 2)], 6, y_high)
    down_w = share(fc.at[y, pl.ds(1, 2)], fc.at[y, pl.ds(1, 2)], 7, y_low)
    interpolate([1], [y], packed, inverse, cells, weights, pred)
    up_last.wait_recv()
    down_last.wait_recv()
    pack_block(y_low, fc, packed, inverse)
    pack_block(y_high, fc, packed, inverse)
    pass_up.wait_recv()
    pass_down.wait_recv()
    pack_block(y_far, fc, packed, inverse)
    interpolate([0, 1], [y_low, y_high, y_far], packed, inverse, cells, weights, pred)
    up_w.wait_recv()
    down_w.wait_recv()
    pass_u = share(fc.at[y_low, 1], fc.at[y_low, 1], 8, y_high)
    pass_v = share(fc.at[y_high, 2], fc.at[y_high, 2], 9, y_low)
    hear(7)

    everyone = tab.at[pl.ds(0, NS - 1)]
    pltpu.make_async_copy(everyone, everyone, tab_recv).wait()
    scale = math.sqrt((M - 1) / N_OBS)
    @pl.loop(0, BLK)
    def _(b):
        t = target[b]
        seen = tab[t // 2, 0, pl.ds(t % 2, 1), :]
        factor = tab[t // 2, 1, pl.ds(t % 2, 1), :] * scale
        parts = [pred[yb, b] for yb in range(NM)]
        middle = jnp.sum(parts[0] + parts[1] + parts[2] + parts[3], axis=0, keepdims=True) * (1.0 / M)
        at = pl.ds(pl.multiple_of(b * OBS, OBS), OBS)
        for yb in range(NM):
            X[yb * LM : (yb + 1) * LM, at] = (parts[yb] - middle) * factor
        X[M : M + 1, at] = (seen - middle) * factor

    gram = lax.dot_general(
        X[0:M], X[...], (((1,), (1,)), ((), ())), precision=HIGHEST, preferred_element_type=jnp.float32
    )
    for q in range(GROUP):
        Gs[q] = gram[2 * q : 2 * q + 2]
    for q, peer in members:
        pltpu.make_async_remote_copy(
            src_ref=Gs.at[q], dst_ref=rs.at[place], send_sem=red_send.at[0], recv_sem=red_recv.at[0],
            device_id=peer, device_id_type=MESH,
        ).start()

    rs[place] = Gs[place]
    others = rs.at[pl.ds(0, GROUP - 1)]
    pltpu.make_async_copy(others, others, red_recv.at[0]).wait()
    mine = tree_sum([rs[q] for q in range(GROUP)])
    zs[...] = mine
    zb[z] = mine
    for peer in ring:
        pltpu.make_async_remote_copy(
            src_ref=zs, dst_ref=zb.at[z], send_sem=red_send.at[1], recv_sem=red_recv.at[1],
            device_id=peer, device_id_type=MESH,
        ).start()

    others_z = zb.at[pl.ds(0, NZ - 1)]
    pltpu.make_async_copy(others_z, others_z, red_recv.at[1]).wait()
    ga[place] = tree_sum([zb[q] for q in range(NZ)])
    for q, peer in members:
        pltpu.make_async_remote_copy(
            src_ref=ga.at[place], dst_ref=ga.at[place], send_sem=red_send.at[2], recv_sem=red_recv.at[2],
            device_id=peer, device_id_type=MESH,
        ).start()

    pltpu.make_async_copy(others, others, red_send.at[0]).wait()
    pltpu.make_async_copy(others_z, others_z, red_send.at[1]).wait()
    others_a = ga.at[pl.ds(0, GROUP - 1)]
    pltpu.make_async_copy(others_a, others_a, red_recv.at[2]).wait()
    pltpu.make_async_copy(others_a, others_a, red_send.at[2]).wait()
    for q in range(GROUP):
        total[2 * q : 2 * q + 2] = ga[q]
    pass_u.wait_recv()
    pass_v.wait_recv()
    for copy in (up_first, down_first, up_last, down_last, pass_up, pass_down, up_w, down_w, pass_u, pass_v):
        copy.wait_send()
    pltpu.make_async_copy(everyone, everyone, tab_send).wait()


def inverse_factor(g):
    sub = lax.broadcasted_iota(jnp.int32, (8, 2 * M), 0)
    lane = lax.broadcasted_iota(jnp.int32, (8, 2 * M), 1)
    work = []
    for n in range(M // 8):
        diagonal = jnp.where(lane == sub + 8 * n, float(M - 1), 0.0)
        right = jnp.where(lane == sub + 8 * n + M, 1.0, 0.0)
        work.append(jnp.where(lane < M, g[8 * n : 8 * n + 8] + diagonal, right))

    def spread(row):
        return jnp.broadcast_to(row, (8, 2 * M))

    result = []
    for n in range(M // 8):
        below = range(n, M // 8)
        column = [{r: spread(work[r][:, 8 * n + j : 8 * n + j + 1]) for r in below} for j in range(8)]
        pivots = jnp.zeros((8, 2 * M), jnp.float32)
        for j in range(8):
            pivot = spread(column[j][n][j : j + 1])
            pivots = jnp.where(sub == j, pivot, pivots)
            inverse = 1.0 / pivot
            ratio = {r: column[j][r] * inverse for r in below}
            ratio[n] = jnp.where(sub > j, ratio[n], 0.0)
            for k in range(j + 1, 8):
                head = spread(column[k][n][j : j + 1])
                for r in below:
                    column[k][r] = column[k][r] - ratio[r] * head
            row = spread(work[n][j : j + 1])
            for r in below:
                work[r] = work[r] - ratio[r] * row
        result.append(jnp.where(lane >= M, work[n] * (1.0 / jnp.sqrt(pivots)), 0.0))
    return jnp.concatenate(result, axis=0)


def two_terms(value):
    high = value.astype(jnp.bfloat16)
    return high, (value - high.astype(jnp.float32)).astype(jnp.bfloat16)


def combine_kernel(total, fc, out, inv_ref, held, sem):
    y = lax.axis_index("mem")
    g = total[...]
    lower_inv = inverse_factor(g)
    inv_ref[...] = lower_inv
    row = lax.broadcasted_iota(jnp.int32, (M, 2 * M), 0)
    lane = lax.broadcasted_iota(jnp.int32, (M, 2 * M), 1)
    square = jnp.where(lane == row + M, jnp.broadcast_to(g[:, M : M + 1], (M, 2 * M)), 0.0)
    proj_row = jnp.broadcast_to(jnp.sum(square, axis=0, keepdims=True), (8, 2 * M))
    first = lax.dot_general(
        proj_row, lower_inv, (((1,), (1,)), ((), ())), precision=HIGHEST, preferred_element_type=jnp.float32
    )
    mean_weights = jnp.dot(first, lower_inv, precision=HIGHEST, preferred_element_type=jnp.float32)[0:1]
    coef = mean_weights + math.sqrt(M - 1) * inv_ref[pl.ds(pl.multiple_of(y * LM, LM), LM), :]
    mixing = (coef + (1.0 - jnp.sum(coef, axis=1, keepdims=True)) * (1.0 / M))[:, M:]
    mix_high, mix_low = two_terms(mixing)
    mix = jnp.concatenate([mix_high, mix_high, mix_low], axis=1)
    for f in range(3):

        @pl.loop(0, ROWS, unroll=ROWS)
        def _(r):
            high, low = two_terms(jnp.concatenate([fc[yb, f, r] for yb in range(NM)], axis=0))
            prior = jnp.concatenate([high, low, high], axis=0)
            new = jnp.dot(mix, prior, preferred_element_type=jnp.float32)
            for c in range(2):
                held[c, pl.ds(f * ROWS + r, LM, stride=3 * ROWS), :] = new[:, c * OBS : (c + 1) * OBS]

    stores = [pltpu.make_async_copy(held.at[c], out.at[:, pl.ds(c * OBS, OBS)], sem.at[c]) for c in range(2)]
    for store in stores:
        store.start()
    for store in stores:
        store.wait()


def local(state, depth, obs_cells, obs_weights, owner_map, obs_values, obs_precision):
    any_space = pl.BlockSpec(memory_space=pltpu.HBM)
    f32 = jnp.float32
    fc, total = pl.pallas_call(
        main_kernel,
        name="forecast_and_reduce",
        out_shape=(
            jax.ShapeDtypeStruct((NM, 3, ROWS, LM, COLS), f32),
            jax.ShapeDtypeStruct((M, 2 * M), f32),
        ),
        in_specs=[any_space] * 7,
        out_specs=(pl.BlockSpec(memory_space=pltpu.VMEM), pl.BlockSpec(memory_space=pltpu.VMEM)),
        scratch_shapes=[
            pltpu.SMEM((8192 // NS,), jnp.int32),
            pltpu.SMEM((BLK,), jnp.int32),
            pltpu.VMEM((2, LM * 3 * ROWS, OBS), f32),
            pltpu.VMEM((ROWS, COLS), f32),
            pltpu.VMEM((4, BLK, OBS), jnp.int32),
            pltpu.VMEM((4, BLK, OBS), f32),
            pltpu.VMEM((3, EXT, LM, COLS), f32),
            pltpu.VMEM((EXT, 8, COLS), f32),
            pltpu.VMEM((EXT, LM, COLS), f32),
            pltpu.VMEM((EXT, LM, COLS), f32),
            pltpu.VMEM((EXT, LM, COLS), f32),
            pltpu.VMEM((EXT, LM, COLS), f32),
            pltpu.VMEM((NM, ROWS, 8, COLS), jnp.int32),
            pltpu.VMEM((NM, LM, OBS), f32),
            pltpu.VMEM((NM, BLK, LM, OBS), f32),
            pltpu.VMEM((2 * M, BLK * OBS), f32),
            pltpu.VMEM((NS, 2, 2, OBS), f32),
            pltpu.VMEM((NS, 2, 2, OBS), f32),
            pltpu.VMEM((GROUP, 2, 2 * M), f32),
            pltpu.VMEM((GROUP, 2, 2 * M), f32),
            pltpu.VMEM((2, 2 * M), f32),
            pltpu.VMEM((NZ, 2, 2 * M), f32),
            pltpu.VMEM((GROUP, 2, 2 * M), f32),
            pltpu.SemaphoreType.DMA((8,)),
            pltpu.SemaphoreType.DMA((2, 3)),
            pltpu.SemaphoreType.DMA((2, 3)),
            pltpu.SemaphoreType.DMA((10,)),
            pltpu.SemaphoreType.DMA((10,)),
            pltpu.SemaphoreType.DMA,
            pltpu.SemaphoreType.DMA,
            pltpu.SemaphoreType.DMA((3,)),
            pltpu.SemaphoreType.DMA((3,)),
            pltpu.SemaphoreType.REGULAR((8,)),
        ],
        compiler_params=pltpu.CompilerParams(collective_id=0, has_side_effects=True, vmem_limit_bytes=40 << 20),
    )(
        *(
            pltpu.with_memory_space_constraint(a, pltpu.HBM)
            for a in (
                owner_map.reshape(-1), state.reshape(LM * 3 * ROWS, COLS), depth,
                obs_cells, obs_weights, obs_values, obs_precision,
            )
        )
    )
    vmem = pl.BlockSpec(memory_space=pltpu.VMEM)
    out = pl.pallas_call(
        combine_kernel,
        name="combine_members",
        out_shape=jax.ShapeDtypeStruct((LM * 3 * ROWS, COLS), f32),
        in_specs=[vmem, vmem],
        out_specs=any_space,
        scratch_shapes=[
            pltpu.VMEM((M, 2 * M), f32),
            pltpu.VMEM((2, LM * 3 * ROWS, OBS), f32),
            pltpu.SemaphoreType.DMA((2,)),
        ],
        compiler_params=pltpu.CompilerParams(vmem_limit_bytes=40 << 20),
    )(total, fc)
    return out.reshape(LM, 3, ROWS, COLS)


def solution(mesh):
    return jax.shard_map(
        local,
        mesh=mesh,
        in_specs=(
            P("mem", None, "space", None),
            P("space", None),
            P(None, "space", None),
            P(None, "space", None),
            P("space", None),
            P("space", None, None, None),
            P("space", None, None, None),
        ),
        out_specs=P("mem", None, "space", None),
        check_vma=False,
    )
```

```python
import math

import jax
import jax.numpy as jnp
from jax import lax
from jax.experimental import pallas as pl
from jax.experimental.pallas import tpu as pltpu
from jax.sharding import PartitionSpec as P

M = 64
NS = 128
NM = 4
NZ = 16
GROUP = 32
LM = M // NM
ROWS = 16
COLS = 256
HALO = 4
EXT = ROWS + 2 * HALO
BLK = 16
OBS = 128
N_OBS = 8192 * 128
GROUPS = (slice(0, 8), slice(8, 16))
EAST, HEIGHT, NORTH = 0, 1, 2
FIELD = (HEIGHT, EAST, NORTH)
MESH = pl.DeviceIdType.MESH
mass_rate = 0.2
wave_rate = 0.2
turn_rate = 0.1


def east(field):
    return pltpu.roll(field, COLS - 1, 1)


def west(field):
    return pltpu.roll(field, 1, 1)


def height_step(i, keep, S, DB, H1):
    for g in GROUPS:
        flux = DB[i] * S[NORTH, i, g]
        change = DB[i + 1] * S[EAST, i + 1, g] - DB[i - 1] * S[EAST, i - 1, g] + (east(flux) - west(flux))
        H1[i, g] = (S[HEIGHT, i, g] - mass_rate * change) * keep


def wind_step(i, S, H1, U1, V1):
    for g in GROUPS:
        u, v, h = S[EAST, i, g], S[NORTH, i, g], H1[i, g]
        U1[i, g] = u - wave_rate * (H1[i + 1, g] - H1[i - 1, g]) + turn_rate * v
        V1[i, g] = v - wave_rate * (east(h) - west(h)) - turn_rate * u


def second_height(i, keep, DB, H1, U1, V1, H2):
    for g in GROUPS:
        flux = DB[i] * V1[i, g]
        change = DB[i + 1] * U1[i + 1, g] - DB[i - 1] * U1[i - 1, g] + (east(flux) - west(flux))
        H2[i, g] = (H1[i, g] - mass_rate * change) * keep


def pack_block(yb, height, packed, inverse):
    top = lax.fori_loop(
        0, ROWS, lambda r, t: jnp.maximum(t, jnp.abs(height(r))), jnp.zeros((LM, COLS), jnp.float32), unroll=4
    )
    top = jnp.maximum(jnp.max(top, axis=1, keepdims=True), 1e-30)
    scale = 32000.0 / top
    inverse[yb] = jnp.broadcast_to(top * (1.0 / 32000.0), (LM, OBS))

    @pl.loop(0, ROWS, unroll=4)
    def _(r):
        q = jnp.floor(height(r) * scale + 0.5).astype(jnp.int32)
        packed[yb, r] = (q[0:8] << 16) | (q[8:16] & 0xFFFF)


def interpolate(half, span, blocks, packed, inverse, cells, weights, pred):
    @pl.loop(*span)
    def _(b):
        lane, chunk, weight = [], [], []
        for k in range(2):
            cell = jnp.broadcast_to(cells[half * 2 + k, pl.ds(b, 1), :], (8, OBS))
            lane.append(cell & (OBS - 1))
            chunk.append(cell >> 7)
            weight.append(jnp.broadcast_to(weights[half * 2 + k, pl.ds(b, 1), :], (8, OBS)))
        held = [[jnp.zeros((8, OBS), jnp.int32) for _ in blocks] for _ in range(2)]
        for c in range(ROWS * COLS // OBS):
            row, col = c // 2, (c % 2) * OBS
            here = [chunk[k] == c for k in range(2)]
            for g, yb in enumerate(blocks):
                values = packed[yb, row, :, col : col + OBS]
                for k in range(2):
                    found = jnp.take_along_axis(values, lane[k], axis=1, mode="promise_in_bounds")
                    held[k][g] = jnp.where(here[k], found, held[k][g])
        for g, yb in enumerate(blocks):
            high = sum((held[k][g] >> 16).astype(jnp.float32) * weight[k] for k in range(2))
            low = sum(((held[k][g] << 16) >> 16).astype(jnp.float32) * weight[k] for k in range(2))
            part = jnp.concatenate([high, low], axis=0) * inverse[yb]
            pred[yb, b] = part if half == 0 else pred[yb, b] + part


def two_terms(value):
    high = value.astype(jnp.bfloat16)
    return high, (value - high.astype(jnp.float32)).astype(jnp.bfloat16)


def tree_sum(terms):
    while len(terms) > 1:
        terms = [sum(terms[i : i + 2][1:], terms[i]) for i in range(0, len(terms), 2)]
    return terms[0]


def main_kernel(
    owners_hbm, state, depth, cells_hbm, weights_hbm, values, precisions, fc, total,
    owners, st, dp, cells, weights, S, DB, H1, U1, V1, H2, packed, inverse, pred, XH, XL, sent, tab, picked, given, Gs, rs, zs, zb, ga,
    load_sem, halo_send, halo_recv, ag_send, ag_recv, tab_send, tab_recv, red_send, red_recv, round_sem, pick_send, pick_recv,
):
    s = lax.axis_index("space")
    y = lax.axis_index("mem")
    core = s % 2
    z = (s // 2) % NZ
    x = s // (2 * NZ)
    y_low, y_high, y_far = (y + 3) % NM, (y + 1) % NM, (y + 2) % NM
    place = (x * NM + y) * 2 + core
    left, right = (s + NS - 1) % NS, (s + 1) % NS

    def along_z(step):
        return (x * (2 * NZ) + ((z + step + NZ) % NZ) * 2 + core, y)

    def along_x(step):
        return (((x + step + 4) % 4) * (2 * NZ) + z * 2 + core, y)

    def along_y(step):
        return (s, (y + step + NM) % NM)

    partner = (s + 1 - 2 * core, y)

    def beside(dx, dy, dc):
        nx, ny, nc = (x + dx) % 4, (y + dy) % NM, core + dc - 2 * dc * core
        return (nx * NM + ny) * 2 + nc, (nx * (2 * NZ) + z * 2 + nc, ny)

    def hops(k, size):
        return min(k, size - k)

    steps = sorted(
        ((dx, dy, dc) for dx in range(4) for dy in range(NM) for dc in range(2) if (dx, dy, dc) != (0, 0, 0)),
        key=lambda d: -(hops(d[0], 4) + hops(d[1], NM)),
    )
    members = [beside(*step) for step in steps]
    ring = [along_z(k) for k in sorted(range(1, NZ), key=lambda k: -hops(k, NZ))]
    own_rows = pl.ds(pl.multiple_of(y * BLK, BLK), BLK)
    loads = [
        pltpu.make_async_copy(state.at[:, pl.ds(0, OBS)], st.at[0], load_sem.at[0]),
        pltpu.make_async_copy(state.at[:, pl.ds(OBS, OBS)], st.at[1], load_sem.at[1]),
        pltpu.make_async_copy(depth, dp, load_sem.at[2]),
        pltpu.make_async_copy(cells_hbm.at[:, own_rows], cells, load_sem.at[3]),
        pltpu.make_async_copy(weights_hbm.at[:, own_rows], weights, load_sem.at[4]),
        pltpu.make_async_copy(owners_hbm, owners, load_sem.at[5]),
        pltpu.make_async_copy(values.at[0], sent.at[:, 0], load_sem.at[6]),
        pltpu.make_async_copy(precisions.at[0], sent.at[:, 1], load_sem.at[7]),
    ]
    for load in loads:
        load.start()

    barrier = pltpu.get_barrier_semaphore()
    cross = (left + core * (right - left), y)
    near = [partner, cross, along_z(1), along_z(-1), along_x(1), along_x(-1), along_y(1), along_y(-1)]
    for peer in near:
        pl.semaphore_signal(barrier, inc=1, device_id=peer, device_id_type=MESH)

    rounds = [
        (along_z(1), along_z(-1)),
        (along_z(2), along_z(-2)),
        (along_z(4), along_z(-4)),
        (partner,),
        (along_x(1), along_x(-1)),
        (along_x(1), along_x(-1)),
        (along_y(1), along_y(-1)),
        (along_y(1), along_y(-1)),
    ]

    def tell(n):
        for peer in rounds[n]:
            pl.semaphore_signal(round_sem.at[n], inc=1, device_id=peer, device_id_type=MESH)

    def hear(n):
        pl.semaphore_wait(round_sem.at[n], len(rounds[n]))

    for terms in (XH, XL):
        terms[M : 2 * M] = jnp.zeros((M, BLK * OBS), jnp.bfloat16)
    for load in loads[:3]:
        load.wait()
    for f in range(3):
        for r in range(ROWS):
            for c in range(2):
                S[FIELD[f], HALO + r, :, c * OBS : (c + 1) * OBS] = st[c, pl.ds(f * ROWS + r, LM, stride=3 * ROWS), :]
    for r in range(ROWS):
        DB[HALO + r] = jnp.broadcast_to(dp[pl.ds(r, 1), :], (8, COLS))
    pl.semaphore_wait(barrier, len(near))

    halos = []
    for n, (peer, src, dst) in enumerate(((left, HALO, HALO + ROWS), (right, ROWS, 0))):
        for k, (buf, lead, skip, rows) in enumerate(
            ((S, (EAST,), 0, HALO), (S, (pl.ds(HEIGHT, 2),), n, HALO - 1), (DB, (), 0, HALO))
        ):
            halos.append(
                pltpu.make_async_remote_copy(
                    src_ref=buf.at[(*lead, pl.ds(src + skip, rows))], dst_ref=buf.at[(*lead, pl.ds(dst + skip, rows))],
                    send_sem=halo_send.at[n, k], recv_sem=halo_recv.at[n, k], device_id=(peer, y), device_id_type=MESH,
                )
            )
            halos[-1].start()

    tell(0)

    @pl.loop(HALO + 1, HALO + ROWS - 1, unroll=2)
    def _(i):
        height_step(i, 1.0, S, DB, H1)

    @pl.loop(HALO + 2, HALO + ROWS - 2, unroll=2)
    def _(i):
        wind_step(i, S, H1, U1, V1)

    hear(0)
    tell(1)

    @pl.loop(HALO + 3, HALO + ROWS - 3, unroll=2)
    def _(i):
        second_height(i, 1.0, DB, H1, U1, V1, H2)

    for halo in halos:
        halo.wait_recv()

    inside_low = jnp.where(s > 0, 1.0, 0.0).astype(jnp.float32)
    inside_high = jnp.where(s < NS - 1, 1.0, 0.0).astype(jnp.float32)
    for i in range(HALO):
        DB[i] = DB[i] * inside_low
        DB[HALO + ROWS + i] = DB[HALO + ROWS + i] * inside_high
    for i in range(1, 5):
        height_step(i, inside_low if i < HALO else 1.0, S, DB, H1)
        height_step(EXT - 1 - i, inside_high if i < HALO else 1.0, S, DB, H1)
    hear(1)
    tell(2)
    for i in range(2, 6):
        wind_step(i, S, H1, U1, V1)
        wind_step(EXT - 1 - i, S, H1, U1, V1)
    for i in range(3, 7):
        second_height(i, inside_low if i < HALO else 1.0, DB, H1, U1, V1, H2)
        second_height(EXT - 1 - i, inside_high if i < HALO else 1.0, DB, H1, U1, V1, H2)

    def share(src, dst, n, peer):
        copy = pltpu.make_async_remote_copy(
            src_ref=src, dst_ref=dst, send_sem=ag_send.at[n], recv_sem=ag_recv.at[n],
            device_id=(s, peer), device_id_type=MESH,
        )
        copy.start()
        return copy

    half = ROWS // 2
    first, last = pl.ds(0, half), pl.ds(half, half)
    sent_first, sent_last = H2.at[pl.ds(HALO, half)], H2.at[pl.ds(HALO + half, half)]
    up_first = share(sent_first, fc.at[y, 0, first], 0, y_high)
    down_first = share(sent_last, fc.at[y, 0, last], 1, y_low)
    up_last = share(sent_last, fc.at[y, 0, last], 2, y_high)
    down_last = share(sent_first, fc.at[y, 0, first], 3, y_low)

    loads[3].wait()
    loads[4].wait()
    pack_block(y, lambda r: H2[HALO + r], packed, inverse)
    interpolate(0, (0, BLK), [y], packed, inverse, cells, weights, pred)
    hear(2)
    tell(3)
    interpolate(1, (0, BLK // 2), [y], packed, inverse, cells, weights, pred)
    hear(3)
    tell(4)
    interpolate(1, (BLK // 2, BLK), [y], packed, inverse, cells, weights, pred)
    up_first.wait_recv()
    down_first.wait_recv()
    pass_up = share(fc.at[y_low, 0, first], fc.at[y_low, 0, first], 4, y_high)
    pass_down = share(fc.at[y_high, 0, last], fc.at[y_high, 0, last], 5, y_low)
    hear(4)
    tell(5)

    @pl.loop(HALO, HALO + ROWS, unroll=2)
    def _(i):
        u, v, h = U1[i], V1[i], H2[i]
        fc[y, 1, i - HALO] = u - wave_rate * (H2[i + 1] - H2[i - 1]) + turn_rate * v
        fc[y, 2, i - HALO] = v - wave_rate * (east(h) - west(h)) - turn_rate * u

    loads[6].wait()
    loads[7].wait()
    hear(5)
    tell(6)

    kind, slot = y // 2, y % 2

    def row_for(peer):
        return sent.at[peer, kind, pl.ds(slot, 1)]

    own_row = pltpu.make_async_copy(row_for(s), tab.at[s], load_sem.at[8])
    own_row.start()

    @pl.loop(1, NS)
    def _(i):
        peer = s + i
        peer = peer - jnp.where(peer >= NS, NS, 0)
        pltpu.make_async_remote_copy(
            src_ref=row_for(peer), dst_ref=tab.at[s], send_sem=tab_send, recv_sem=tab_recv,
            device_id=(peer, y), device_id_type=MESH,
        ).start()

    up_last.wait_recv()
    down_last.wait_recv()
    pack_block(y_low, lambda r: fc[y_low, 0, r], packed, inverse)
    pack_block(y_high, lambda r: fc[y_high, 0, r], packed, inverse)
    hear(6)
    tell(7)
    pass_up.wait_recv()
    pass_down.wait_recv()
    up_u = share(fc.at[y, 1], fc.at[y, 1], 6, y_high)
    down_u = share(fc.at[y, 1], fc.at[y, 1], 7, y_low)
    pack_block(y_far, lambda r: fc[y_far, 0, r], packed, inverse)
    rest = [y_low, y_high, y_far]
    interpolate(0, (0, BLK), rest, packed, inverse, cells, weights, pred)
    interpolate(1, (0, BLK // 2), rest, packed, inverse, cells, weights, pred)

    loads[5].wait()
    blocks = 8192 // NS
    across = jnp.broadcast_to(owners[...], (blocks, blocks))
    down_at = lax.broadcasted_iota(jnp.int32, (blocks, blocks), 0)
    across_at = lax.broadcasted_iota(jnp.int32, (blocks, blocks), 1)
    mine_down = jnp.sum(jnp.where(down_at == across_at, across, 0), axis=1, keepdims=True)
    earlier = jnp.where((across == mine_down) & (across_at < down_at), 1, 0)
    slot_down = jnp.sum(earlier, axis=1, keepdims=True)
    wanted = jnp.where(slot_down == slot, mine_down, -1)
    choose = jnp.where(lax.broadcasted_iota(jnp.int32, (blocks, NS), 1) == wanted, 1.0, 0.0).astype(jnp.bfloat16)
    own_row.wait()
    everyone = tab.at[pl.ds(0, NS - 1)]
    pltpu.make_async_copy(everyone, everyone, tab_recv).wait()
    rows = tab[...].reshape(NS, OBS)
    high, low = two_terms(rows)
    left_over = (rows - high.astype(jnp.float32) - low.astype(jnp.float32)).astype(jnp.bfloat16)

    def take(term):
        return jnp.dot(choose, term, preferred_element_type=jnp.float32)

    chosen = take(high) + (take(low) + take(left_over))
    for q in range(NM):
        picked[q] = chosen[q * BLK : (q + 1) * BLK]
    hand = []
    for step in range(1, NM):
        peer = (y + step) % NM
        hand.append(
            pltpu.make_async_remote_copy(
                src_ref=picked.at[peer], dst_ref=given.at[y], send_sem=pick_send.at[step], recv_sem=pick_recv.at[step],
                device_id=(s, peer), device_id_type=MESH,
            )
        )
        hand[-1].start()
    given[y] = picked[y]
    up_v = share(fc.at[y, 2], fc.at[y, 2], 10, y_high)
    down_v = share(fc.at[y, 2], fc.at[y, 2], 11, y_low)
    interpolate(1, (BLK // 2, BLK), rest, packed, inverse, cells, weights, pred)
    hear(7)
    for copy in hand:
        copy.wait_recv()

    scale = math.sqrt((M - 1) / N_OBS)

    def keep_terms(rows, at, value):
        XH[rows, at], XL[rows, at] = two_terms(value)

    @pl.loop(0, BLK)
    def _(b):
        at_block = pl.ds(b, 1)
        seen = given[0, at_block, :] + given[1, at_block, :]
        factor = (given[2, at_block, :] + given[3, at_block, :]) * scale
        parts = [pred[yb, b] for yb in range(NM)]
        middle = jnp.sum(parts[0] + parts[1] + parts[2] + parts[3], axis=0, keepdims=True) * (1.0 / M)
        at = pl.ds(pl.multiple_of(b * OBS, OBS), OBS)
        for yb in range(NM):
            keep_terms(slice(yb * LM, (yb + 1) * LM), at, (parts[yb] - middle) * factor)
        depart = jnp.broadcast_to((seen - middle) * factor, (LM, OBS))
        keep_terms(slice(M, M + LM), at, jnp.where(lax.broadcasted_iota(jnp.int32, (LM, OBS), 0) == 0, depart, 0.0))

    def product(a, b):
        return lax.dot_general(a[0:M], b[...], (((1,), (1,)), ((), ())), preferred_element_type=jnp.float32)

    gram = product(XH, XH) + (product(XH, XL) + product(XL, XH))
    for q in range(GROUP):
        Gs[q] = gram[2 * q : 2 * q + 2]
    for q, peer in members:
        pltpu.make_async_remote_copy(
            src_ref=Gs.at[q], dst_ref=rs.at[place], send_sem=red_send.at[0], recv_sem=red_recv.at[0],
            device_id=peer, device_id_type=MESH,
        ).start()

    rs[place] = Gs[place]

    @pl.loop(0, ROWS, unroll=2)
    def _(r):
        fc[y, 0, r] = H2[HALO + r]

    others = rs.at[pl.ds(0, GROUP - 1)]
    pltpu.make_async_copy(others, others, red_recv.at[0]).wait()
    up_u.wait_recv()
    down_u.wait_recv()
    up_v.wait_recv()
    down_v.wait_recv()
    mine = tree_sum([rs[q] for q in range(GROUP)])
    zs[...] = mine
    zb[z] = mine
    for peer in ring:
        pltpu.make_async_remote_copy(
            src_ref=zs, dst_ref=zb.at[z], send_sem=red_send.at[1], recv_sem=red_recv.at[1],
            device_id=peer, device_id_type=MESH,
        ).start()

    pass_u = share(fc.at[y_low, 1], fc.at[y_low, 1], 8, y_high)
    pass_v = share(fc.at[y_high, 2], fc.at[y_high, 2], 9, y_low)
    others_z = zb.at[pl.ds(0, NZ - 1)]
    pltpu.make_async_copy(others_z, others_z, red_recv.at[1]).wait()
    ga[place] = tree_sum([zb[q] for q in range(NZ)])
    for q, peer in members:
        pltpu.make_async_remote_copy(
            src_ref=ga.at[place], dst_ref=ga.at[place], send_sem=red_send.at[2], recv_sem=red_recv.at[2],
            device_id=peer, device_id_type=MESH,
        ).start()

    pltpu.make_async_copy(others, others, red_send.at[0]).wait()
    pltpu.make_async_copy(others_z, others_z, red_send.at[1]).wait()
    others_a = ga.at[pl.ds(0, GROUP - 1)]
    pltpu.make_async_copy(others_a, others_a, red_recv.at[2]).wait()
    pltpu.make_async_copy(others_a, others_a, red_send.at[2]).wait()
    for q in range(GROUP):
        total[2 * q : 2 * q + 2] = ga[q]
    pass_u.wait_recv()
    pass_v.wait_recv()
    for copy in halos + hand:
        copy.wait_send()
    for copy in (up_first, down_first, up_last, down_last, pass_up, pass_down, up_u, down_u, up_v, down_v, pass_u, pass_v):
        copy.wait_send()
    pltpu.make_async_copy(everyone, everyone, tab_send).wait()


def inverse_factor(g):
    sub = lax.broadcasted_iota(jnp.int32, (8, 2 * M), 0)
    lane = lax.broadcasted_iota(jnp.int32, (8, 2 * M), 1)
    work = []
    for n in range(M // 8):
        diagonal = jnp.where(lane == sub + 8 * n, float(M - 1), 0.0)
        right = jnp.where(lane == sub + 8 * n + M, 1.0, 0.0)
        work.append(jnp.where(lane < M, g[8 * n : 8 * n + 8] + diagonal, right))

    spot = lax.broadcasted_iota(jnp.int32, (M, 2 * M), 0) == lax.broadcasted_iota(jnp.int32, (M, 2 * M), 1)
    proj = jnp.where(spot, jnp.broadcast_to(g[:, M : M + 1], (M, 2 * M)), 0.0)
    work.append(jnp.broadcast_to(jnp.sum(proj, axis=0, keepdims=True), (8, 2 * M)))

    def spread(row):
        return jnp.broadcast_to(row, (8, 2 * M))

    result = []
    for n in range(M // 8):
        below = range(n, M // 8 + 1)
        column = [{r: spread(work[r][:, 8 * n + j : 8 * n + j + 1]) for r in below} for j in range(8)]
        pivots = jnp.zeros((8, 2 * M), jnp.float32)
        for j in range(8):
            pivot = spread(column[j][n][j : j + 1])
            pivots = jnp.where(sub == j, pivot, pivots)
            inverse = 1.0 / pivot
            ratio = {r: column[j][r] * inverse for r in below}
            ratio[n] = jnp.where(sub > j, ratio[n], 0.0)
            for k in range(j + 1, 8):
                head = spread(column[k][n][j : j + 1])
                for r in below:
                    column[k][r] = column[k][r] - ratio[r] * head
            row = spread(work[n][j : j + 1])
            for r in below:
                work[r] = work[r] - ratio[r] * row
        result.append(jnp.where(lane >= M, work[n] * (1.0 / jnp.sqrt(pivots)), 0.0))
    return jnp.concatenate(result, axis=0), -work[M // 8][0:1]


def combine_kernel(total, fc, out, inv_ref, held, sem):
    y = lax.axis_index("mem")
    lower_inv, mean_weights = inverse_factor(total[...])
    inv_ref[...] = lower_inv
    coef = mean_weights + math.sqrt(M - 1) * inv_ref[pl.ds(pl.multiple_of(y * LM, LM), LM), :]
    coef = coef[:, M:]
    mixing = coef + (1.0 - jnp.sum(coef, axis=1, keepdims=True)) * (1.0 / M)
    mix_high, mix_low = two_terms(mixing)
    mix = jnp.concatenate([mix_high, mix_high, mix_low], axis=1)
    for f in range(3):

        @pl.loop(0, ROWS, unroll=ROWS)
        def _(r):
            high, low = two_terms(jnp.concatenate([fc[yb, f, r] for yb in range(NM)], axis=0))
            prior = jnp.concatenate([high, low, high], axis=0)
            new = jnp.dot(mix, prior, preferred_element_type=jnp.float32)
            for c in range(2):
                held[c, pl.ds(f * ROWS + r, LM, stride=3 * ROWS), :] = new[:, c * OBS : (c + 1) * OBS]

    stores = [pltpu.make_async_copy(held.at[c], out.at[:, pl.ds(c * OBS, OBS)], sem.at[c]) for c in range(2)]
    for store in stores:
        store.start()
    for store in stores:
        store.wait()


def local(state, depth, obs_cells, obs_weights, owner_map, obs_values, obs_precision):
    any_space = pl.BlockSpec(memory_space=pltpu.HBM)
    f32 = jnp.float32
    fc, total = pl.pallas_call(
        main_kernel,
        name="forecast_and_reduce",
        out_shape=(
            jax.ShapeDtypeStruct((NM, 3, ROWS, LM, COLS), f32),
            jax.ShapeDtypeStruct((M, 2 * M), f32),
        ),
        in_specs=[any_space] * 7,
        out_specs=(pl.BlockSpec(memory_space=pltpu.VMEM), pl.BlockSpec(memory_space=pltpu.VMEM)),
        scratch_shapes=[
            pltpu.VMEM((1, 8192 // NS), jnp.int32),
            pltpu.VMEM((2, LM * 3 * ROWS, OBS), f32),
            pltpu.VMEM((ROWS, COLS), f32),
            pltpu.VMEM((4, BLK, OBS), jnp.int32),
            pltpu.VMEM((4, BLK, OBS), f32),
            pltpu.VMEM((3, EXT, LM, COLS), f32),
            pltpu.VMEM((EXT, 8, COLS), f32),
            pltpu.VMEM((EXT, LM, COLS), f32),
            pltpu.VMEM((EXT, LM, COLS), f32),
            pltpu.VMEM((EXT, LM, COLS), f32),
            pltpu.VMEM((EXT, LM, COLS), f32),
            pltpu.VMEM((NM, ROWS, 8, COLS), jnp.int32),
            pltpu.VMEM((NM, LM, OBS), f32),
            pltpu.VMEM((NM, BLK, LM, OBS), f32),
            pltpu.VMEM((2 * M, BLK * OBS), jnp.bfloat16),
            pltpu.VMEM((2 * M, BLK * OBS), jnp.bfloat16),
            pltpu.VMEM((NS, 2, 2, OBS), f32),
            pltpu.VMEM((NS, 1, OBS), f32),
            pltpu.VMEM((NM, BLK, OBS), f32),
            pltpu.VMEM((NM, BLK, OBS), f32),
            pltpu.VMEM((GROUP, 2, 2 * M), f32),
            pltpu.VMEM((GROUP, 2, 2 * M), f32),
            pltpu.VMEM((2, 2 * M), f32),
            pltpu.VMEM((NZ, 2, 2 * M), f32),
            pltpu.VMEM((GROUP, 2, 2 * M), f32),
            pltpu.SemaphoreType.DMA((9,)),
            pltpu.SemaphoreType.DMA((2, 3)),
            pltpu.SemaphoreType.DMA((2, 3)),
            pltpu.SemaphoreType.DMA((12,)),
            pltpu.SemaphoreType.DMA((12,)),
            pltpu.SemaphoreType.DMA,
            pltpu.SemaphoreType.DMA,
            pltpu.SemaphoreType.DMA((3,)),
            pltpu.SemaphoreType.DMA((3,)),
            pltpu.SemaphoreType.REGULAR((8,)),
            pltpu.SemaphoreType.DMA((NM,)),
            pltpu.SemaphoreType.DMA((NM,)),
        ],
        compiler_params=pltpu.CompilerParams(collective_id=0, has_side_effects=True, vmem_limit_bytes=40 << 20),
    )(
        *(
            pltpu.with_memory_space_constraint(a, pltpu.HBM)
            for a in (
                owner_map.reshape(1, -1), state.reshape(LM * 3 * ROWS, COLS), depth,
                obs_cells, obs_weights, obs_values, obs_precision,
            )
        )
    )
    vmem = pl.BlockSpec(memory_space=pltpu.VMEM)
    out = pl.pallas_call(
        combine_kernel,
        name="combine_members",
        out_shape=jax.ShapeDtypeStruct((LM * 3 * ROWS, COLS), f32),
        in_specs=[vmem, vmem],
        out_specs=any_space,
        scratch_shapes=[
            pltpu.VMEM((M, 2 * M), f32),
            pltpu.VMEM((2, LM * 3 * ROWS, OBS), f32),
            pltpu.SemaphoreType.DMA((2,)),
        ],
        compiler_params=pltpu.CompilerParams(vmem_limit_bytes=40 << 20),
    )(total, fc)
    return out.reshape(LM, 3, ROWS, COLS)


def solution(mesh):
    return jax.shard_map(
        local,
        mesh=mesh,
        in_specs=(
            P("mem", None, "space", None),
            P("space", None),
            P(None, "space", None),
            P(None, "space", None),
            P("space", None),
            P("space", None, None, None),
            P("space", None, None, None),
        ),
        out_specs=P("mem", None, "space", None),
        check_vma=False,
    )
```

```python
import math

import jax
import jax.numpy as jnp
from jax import lax
from jax.experimental import pallas as pl
from jax.experimental.pallas import tpu as pltpu
from jax.sharding import PartitionSpec as P

M = 64
NS = 128
NM = 4
NZ = 16
GROUP = 32
LM = M // NM
ROWS = 16
COLS = 256
HALO = 4
EXT = ROWS + 2 * HALO
BLK = 16
OBS = 128
N_OBS = 8192 * 128
GROUPS = (slice(0, 8), slice(8, 16))
EAST, HEIGHT, NORTH = 0, 1, 2
FIELD = (HEIGHT, EAST, NORTH)
MESH = pl.DeviceIdType.MESH
mass_rate = 0.2
wave_rate = 0.2
turn_rate = 0.1


def east(field):
    return pltpu.roll(field, COLS - 1, 1)


def west(field):
    return pltpu.roll(field, 1, 1)


def height_step(i, keep, S, DB, H1):
    for g in GROUPS:
        flux = DB[i] * S[NORTH, i, g]
        change = DB[i + 1] * S[EAST, i + 1, g] - DB[i - 1] * S[EAST, i - 1, g] + (east(flux) - west(flux))
        H1[i, g] = (S[HEIGHT, i, g] - mass_rate * change) * keep


def wind_step(i, S, H1, U1, V1):
    for g in GROUPS:
        u, v, h = S[EAST, i, g], S[NORTH, i, g], H1[i, g]
        U1[i, g] = u - wave_rate * (H1[i + 1, g] - H1[i - 1, g]) + turn_rate * v
        V1[i, g] = v - wave_rate * (east(h) - west(h)) - turn_rate * u


def second_height(i, keep, DB, H1, U1, V1, H2):
    for g in GROUPS:
        flux = DB[i] * V1[i, g]
        change = DB[i + 1] * U1[i + 1, g] - DB[i - 1] * U1[i - 1, g] + (east(flux) - west(flux))
        H2[i, g] = (H1[i, g] - mass_rate * change) * keep


def pack_block(yb, height, packed, inverse):
    top = lax.fori_loop(
        0, ROWS, lambda r, t: jnp.maximum(t, jnp.abs(height(r))), jnp.zeros((LM, COLS), jnp.float32), unroll=4
    )
    top = jnp.maximum(jnp.max(top, axis=1, keepdims=True), 1e-30)
    scale = 32000.0 / top
    inverse[yb] = jnp.broadcast_to(top * (1.0 / 32000.0), (LM, OBS))

    @pl.loop(0, ROWS, unroll=4)
    def _(r):
        q = jnp.floor(height(r) * scale + 0.5).astype(jnp.int32)
        packed[yb, r] = (q[0:8] << 16) | (q[8:16] & 0xFFFF)


def interpolate(half, span, blocks, packed, inverse, cells, weights, pred):
    @pl.loop(*span)
    def _(b):
        lane, chunk, weight = [], [], []
        for k in range(2):
            cell = jnp.broadcast_to(cells[half * 2 + k, pl.ds(b, 1), :], (8, OBS))
            lane.append(cell & (OBS - 1))
            chunk.append(cell >> 7)
            weight.append(jnp.broadcast_to(weights[half * 2 + k, pl.ds(b, 1), :], (8, OBS)))
        held = [[jnp.zeros((8, OBS), jnp.int32) for _ in blocks] for _ in range(2)]
        for c in range(ROWS * COLS // OBS):
            row, col = c // 2, (c % 2) * OBS
            here = [chunk[k] == c for k in range(2)]
            for g, yb in enumerate(blocks):
                values = packed[yb, row, :, col : col + OBS]
                for k in range(2):
                    found = jnp.take_along_axis(values, lane[k], axis=1, mode="promise_in_bounds")
                    held[k][g] = jnp.where(here[k], found, held[k][g])
        for g, yb in enumerate(blocks):
            high = sum((held[k][g] >> 16).astype(jnp.float32) * weight[k] for k in range(2))
            low = sum(((held[k][g] << 16) >> 16).astype(jnp.float32) * weight[k] for k in range(2))
            part = jnp.concatenate([high, low], axis=0) * inverse[yb]
            pred[yb, b] = part if half == 0 else pred[yb, b] + part


def two_terms(value):
    high = value.astype(jnp.bfloat16)
    return high, (value - high.astype(jnp.float32)).astype(jnp.bfloat16)


def tree_sum(terms):
    while len(terms) > 1:
        terms = [sum(terms[i : i + 2][1:], terms[i]) for i in range(0, len(terms), 2)]
    return terms[0]


def main_kernel(
    owners_hbm, state, depth, cells_hbm, weights_hbm, values, precisions, fc, total,
    owners, st, dp, dp_edge, cells, weights, S, DB, H1, U1, V1, H2, packed, inverse, pred, XH, XL, sent, tab, picked, given, Gs, rs, zs, zb, ga,
    load_sem, halo_send, halo_recv, ag_send, ag_recv, tab_send, tab_recv, red_send, red_recv, round_sem, pick_send, pick_recv,
):
    s = lax.axis_index("space")
    y = lax.axis_index("mem")
    core = s % 2
    z = (s // 2) % NZ
    x = s // (2 * NZ)
    y_low, y_high, y_far = (y + 3) % NM, (y + 1) % NM, (y + 2) % NM
    place = (x * NM + y) * 2 + core
    left, right = (s + NS - 1) % NS, (s + 1) % NS

    def along_z(step):
        return (x * (2 * NZ) + ((z + step + NZ) % NZ) * 2 + core, y)

    def along_x(step):
        return (((x + step + 4) % 4) * (2 * NZ) + z * 2 + core, y)

    def along_y(step):
        return (s, (y + step + NM) % NM)

    partner = (s + 1 - 2 * core, y)

    def beside(dx, dy, dc):
        nx, ny, nc = (x + dx) % 4, (y + dy) % NM, core + dc - 2 * dc * core
        return (nx * NM + ny) * 2 + nc, (nx * (2 * NZ) + z * 2 + nc, ny)

    def hops(k, size):
        return min(k, size - k)

    steps = sorted(
        ((dx, dy, dc) for dx in range(4) for dy in range(NM) for dc in range(2) if (dx, dy, dc) != (0, 0, 0)),
        key=lambda d: -(hops(d[0], 4) + hops(d[1], NM)),
    )
    members = [beside(*step) for step in steps]
    ring = [along_z(k) for k in sorted(range(1, NZ), key=lambda k: -hops(k, NZ))]
    own_rows = pl.ds(pl.multiple_of(y * BLK, BLK), BLK)
    loads = [
        pltpu.make_async_copy(state.at[:, pl.ds(0, OBS)], st.at[0], load_sem.at[0]),
        pltpu.make_async_copy(state.at[:, pl.ds(OBS, OBS)], st.at[1], load_sem.at[1]),
        pltpu.make_async_copy(depth, dp, load_sem.at[2]),
        pltpu.make_async_copy(cells_hbm.at[:, own_rows], cells, load_sem.at[3]),
        pltpu.make_async_copy(weights_hbm.at[:, own_rows], weights, load_sem.at[4]),
        pltpu.make_async_copy(owners_hbm, owners, load_sem.at[5]),
        pltpu.make_async_copy(values.at[0], sent.at[:, 0], load_sem.at[6]),
        pltpu.make_async_copy(precisions.at[0], sent.at[:, 1], load_sem.at[7]),
    ]
    for load in loads:
        load.start()

    barrier = pltpu.get_barrier_semaphore()
    cross = (left + core * (right - left), y)
    near = [partner, cross, along_z(1), along_z(-1), along_x(1), along_x(-1), along_y(1), along_y(-1)]
    for peer in near:
        pl.semaphore_signal(barrier, inc=1, device_id=peer, device_id_type=MESH)

    rounds = [
        (along_z(1), along_z(-1)),
        (along_z(2), along_z(-2)),
        (along_z(4), along_z(-4)),
        (partner,),
        (along_x(1), along_x(-1)),
        (along_x(1), along_x(-1)),
        (along_y(1), along_y(-1)),
        (along_y(1), along_y(-1)),
    ]

    def tell(n):
        for peer in rounds[n]:
            pl.semaphore_signal(round_sem.at[n], inc=1, device_id=peer, device_id_type=MESH)

    def hear(n):
        pl.semaphore_wait(round_sem.at[n], len(rounds[n]))

    for terms in (XH, XL):
        terms[M : 2 * M] = jnp.zeros((M, BLK * OBS), jnp.bfloat16)
    for load in loads[:3]:
        load.wait()
    for f in range(3):
        for r in range(ROWS):
            for c in range(2):
                S[FIELD[f], HALO + r, :, c * OBS : (c + 1) * OBS] = st[c, pl.ds(f * ROWS + r, LM, stride=3 * ROWS), :]
    for r in range(ROWS):
        DB[HALO + r] = jnp.broadcast_to(dp[pl.ds(r, 1), :], (8, COLS))
    pl.semaphore_wait(barrier, len(near))

    halos = []
    for n, (peer, src, dst) in enumerate(((left, HALO, HALO + ROWS), (right, ROWS, 0))):
        for k, (buf, lead, skip, rows) in enumerate(
            ((S, (EAST,), 0, HALO), (S, (pl.ds(HEIGHT, 2),), n, HALO - 1))
        ):
            halos.append(
                pltpu.make_async_remote_copy(
                    src_ref=buf.at[(*lead, pl.ds(src + skip, rows))], dst_ref=buf.at[(*lead, pl.ds(dst + skip, rows))],
                    send_sem=halo_send.at[n, k], recv_sem=halo_recv.at[n, k], device_id=(peer, y), device_id_type=MESH,
                )
            )
            halos[-1].start()

    for n, (peer, src) in enumerate(((left, 0), (right, 8))):
        halos.append(
            pltpu.make_async_remote_copy(
                src_ref=dp.at[pl.ds(src, 8)], dst_ref=dp_edge.at[1 - n], send_sem=halo_send.at[n, 2], recv_sem=halo_recv.at[n, 2],
                device_id=(peer, y), device_id_type=MESH,
            )
        )
        halos[-1].start()

    tell(0)

    @pl.loop(HALO + 1, HALO + ROWS - 1, unroll=2)
    def _(i):
        height_step(i, 1.0, S, DB, H1)

    @pl.loop(HALO + 2, HALO + ROWS - 2, unroll=2)
    def _(i):
        wind_step(i, S, H1, U1, V1)

    hear(0)
    tell(1)

    @pl.loop(HALO + 3, HALO + ROWS - 3, unroll=2)
    def _(i):
        second_height(i, 1.0, DB, H1, U1, V1, H2)

    for halo in halos:
        halo.wait_recv()

    inside_low = jnp.where(s > 0, 1.0, 0.0).astype(jnp.float32)
    inside_high = jnp.where(s < NS - 1, 1.0, 0.0).astype(jnp.float32)
    for i in range(HALO):
        DB[i] = jnp.broadcast_to(dp_edge[0, pl.ds(8 - HALO + i, 1), :], (8, COLS)) * inside_low
        DB[HALO + ROWS + i] = jnp.broadcast_to(dp_edge[1, pl.ds(i, 1), :], (8, COLS)) * inside_high
    for i in range(1, 5):
        height_step(i, inside_low if i < HALO else 1.0, S, DB, H1)
        height_step(EXT - 1 - i, inside_high if i < HALO else 1.0, S, DB, H1)
    hear(1)
    tell(2)
    for i in range(2, 6):
        wind_step(i, S, H1, U1, V1)
        wind_step(EXT - 1 - i, S, H1, U1, V1)
    for i in range(3, 7):
        second_height(i, inside_low if i < HALO else 1.0, DB, H1, U1, V1, H2)
        second_height(EXT - 1 - i, inside_high if i < HALO else 1.0, DB, H1, U1, V1, H2)

    def share(src, dst, n, peer):
        copy = pltpu.make_async_remote_copy(
            src_ref=src, dst_ref=dst, send_sem=ag_send.at[n], recv_sem=ag_recv.at[n],
            device_id=(s, peer), device_id_type=MESH,
        )
        copy.start()
        return copy

    half = ROWS // 2
    first, last = pl.ds(0, half), pl.ds(half, half)
    sent_first, sent_last = H2.at[pl.ds(HALO, half)], H2.at[pl.ds(HALO + half, half)]
    up_first = share(sent_first, fc.at[y, 0, first], 0, y_high)
    down_first = share(sent_last, fc.at[y, 0, last], 1, y_low)
    up_last = share(sent_last, fc.at[y, 0, last], 2, y_high)
    down_last = share(sent_first, fc.at[y, 0, first], 3, y_low)

    loads[3].wait()
    loads[4].wait()
    pack_block(y, lambda r: H2[HALO + r], packed, inverse)
    interpolate(0, (0, BLK), [y], packed, inverse, cells, weights, pred)
    hear(2)
    tell(3)
    interpolate(1, (0, BLK // 2), [y], packed, inverse, cells, weights, pred)
    hear(3)
    tell(4)
    interpolate(1, (BLK // 2, BLK), [y], packed, inverse, cells, weights, pred)
    up_first.wait_recv()
    down_first.wait_recv()
    pass_up = share(fc.at[y_low, 0, first], fc.at[y_low, 0, first], 4, y_high)
    pass_down = share(fc.at[y_high, 0, last], fc.at[y_high, 0, last], 5, y_low)
    hear(4)
    tell(5)

    @pl.loop(HALO, HALO + ROWS, unroll=2)
    def _(i):
        u, v, h = U1[i], V1[i], H2[i]
        fc[y, 1, i - HALO] = u - wave_rate * (H2[i + 1] - H2[i - 1]) + turn_rate * v
        fc[y, 2, i - HALO] = v - wave_rate * (east(h) - west(h)) - turn_rate * u

    loads[6].wait()
    loads[7].wait()
    hear(5)
    tell(6)

    kind, slot = y // 2, y % 2

    def row_for(peer):
        return sent.at[peer, kind, pl.ds(slot, 1)]

    own_row = pltpu.make_async_copy(row_for(s), tab.at[s], load_sem.at[8])
    own_row.start()

    columns = [((x + dx) % 4) * (2 * NZ) + nc for dx in (2, 1, 3, 0) for nc in (1 - core, core)]

    def send_row(peer):
        pltpu.make_async_remote_copy(
            src_ref=row_for(peer), dst_ref=tab.at[s], send_sem=tab_send, recv_sem=tab_recv,
            device_id=(peer, y), device_id_type=MESH,
        ).start()

    @pl.loop(0, NZ - 1)
    def _(k):
        step = (k + 1) // 2
        there = (z + NZ // 2 + jnp.where(k % 2 == 1, step, NZ - step)) % NZ
        for column in columns:
            send_row(column + there * 2)

    for column in columns[:-1]:
        send_row(column + z * 2)

    up_last.wait_recv()
    down_last.wait_recv()
    pack_block(y_low, lambda r: fc[y_low, 0, r], packed, inverse)
    pack_block(y_high, lambda r: fc[y_high, 0, r], packed, inverse)
    hear(6)
    tell(7)
    pass_up.wait_recv()
    pass_down.wait_recv()
    up_u = share(fc.at[y, 1], fc.at[y, 1], 6, y_high)
    down_u = share(fc.at[y, 1], fc.at[y, 1], 7, y_low)
    pack_block(y_far, lambda r: fc[y_far, 0, r], packed, inverse)
    rest = [y_low, y_high, y_far]
    interpolate(0, (0, BLK), rest, packed, inverse, cells, weights, pred)
    interpolate(1, (0, BLK // 4), rest, packed, inverse, cells, weights, pred)

    loads[5].wait()
    blocks = 8192 // NS
    across = jnp.broadcast_to(owners[...], (blocks, blocks))
    down_at = lax.broadcasted_iota(jnp.int32, (blocks, blocks), 0)
    across_at = lax.broadcasted_iota(jnp.int32, (blocks, blocks), 1)
    mine_down = jnp.sum(jnp.where(down_at == across_at, across, 0), axis=1, keepdims=True)
    earlier = jnp.where((across == mine_down) & (across_at < down_at), 1, 0)
    slot_down = jnp.sum(earlier, axis=1, keepdims=True)
    wanted = jnp.where(slot_down == slot, mine_down, -1)
    choose = jnp.where(lax.broadcasted_iota(jnp.int32, (blocks, NS), 1) == wanted, 1.0, 0.0).astype(jnp.bfloat16)
    own_row.wait()
    everyone = tab.at[pl.ds(0, NS - 1)]
    pltpu.make_async_copy(everyone, everyone, tab_recv).wait()
    rows = tab[...].reshape(NS, OBS)
    high, low = two_terms(rows)
    left_over = (rows - high.astype(jnp.float32) - low.astype(jnp.float32)).astype(jnp.bfloat16)

    def take(term):
        return jnp.dot(choose, term, preferred_element_type=jnp.float32)

    chosen = take(high) + (take(low) + take(left_over))
    for q in range(NM):
        picked[q] = chosen[q * BLK : (q + 1) * BLK]
    hand = []
    for step in range(1, NM):
        peer = (y + step) % NM
        hand.append(
            pltpu.make_async_remote_copy(
                src_ref=picked.at[peer], dst_ref=given.at[y], send_sem=pick_send.at[step], recv_sem=pick_recv.at[step],
                device_id=(s, peer), device_id_type=MESH,
            )
        )
        hand[-1].start()
    given[y] = picked[y]
    up_v = share(fc.at[y, 2], fc.at[y, 2], 10, y_high)
    down_v = share(fc.at[y, 2], fc.at[y, 2], 11, y_low)
    interpolate(1, (BLK // 4, BLK), rest, packed, inverse, cells, weights, pred)
    hear(7)
    for copy in hand:
        copy.wait_recv()

    scale = math.sqrt((M - 1) / N_OBS)

    def keep_terms(rows, at, value):
        XH[rows, at], XL[rows, at] = two_terms(value)

    @pl.loop(0, BLK)
    def _(b):
        at_block = pl.ds(b, 1)
        seen = given[0, at_block, :] + given[1, at_block, :]
        factor = (given[2, at_block, :] + given[3, at_block, :]) * scale
        parts = [pred[yb, b] for yb in range(NM)]
        middle = jnp.sum(parts[0] + parts[1] + parts[2] + parts[3], axis=0, keepdims=True) * (1.0 / M)
        at = pl.ds(pl.multiple_of(b * OBS, OBS), OBS)
        for yb in range(NM):
            keep_terms(slice(yb * LM, (yb + 1) * LM), at, (parts[yb] - middle) * factor)
        depart = jnp.broadcast_to((seen - middle) * factor, (LM, OBS))
        keep_terms(slice(M, M + LM), at, jnp.where(lax.broadcasted_iota(jnp.int32, (LM, OBS), 0) == 0, depart, 0.0))

    def product(a, b):
        return lax.dot_general(a[0:M], b[...], (((1,), (1,)), ((), ())), preferred_element_type=jnp.float32)

    gram = product(XH, XH) + (product(XH, XL) + product(XL, XH))
    for q in range(GROUP):
        Gs[q] = gram[2 * q : 2 * q + 2]
    for q, peer in members:
        pltpu.make_async_remote_copy(
            src_ref=Gs.at[q], dst_ref=rs.at[place], send_sem=red_send.at[0], recv_sem=red_recv.at[0],
            device_id=peer, device_id_type=MESH,
        ).start()

    rs[place] = Gs[place]

    @pl.loop(0, ROWS, unroll=2)
    def _(r):
        fc[y, 0, r] = H2[HALO + r]

    others = rs.at[pl.ds(0, GROUP - 1)]
    pltpu.make_async_copy(others, others, red_recv.at[0]).wait()
    up_u.wait_recv()
    down_u.wait_recv()
    up_v.wait_recv()
    down_v.wait_recv()
    mine = tree_sum([rs[q] for q in range(GROUP)])
    zs[...] = mine
    zb[z] = mine
    for peer in ring:
        pltpu.make_async_remote_copy(
            src_ref=zs, dst_ref=zb.at[z], send_sem=red_send.at[1], recv_sem=red_recv.at[1],
            device_id=peer, device_id_type=MESH,
        ).start()

    pass_u = share(fc.at[y_low, 1], fc.at[y_low, 1], 8, y_high)
    pass_v = share(fc.at[y_high, 2], fc.at[y_high, 2], 9, y_low)
    others_z = zb.at[pl.ds(0, NZ - 1)]
    pltpu.make_async_copy(others_z, others_z, red_recv.at[1]).wait()
    ga[place] = tree_sum([zb[q] for q in range(NZ)])
    for q, peer in members:
        pltpu.make_async_remote_copy(
            src_ref=ga.at[place], dst_ref=ga.at[place], send_sem=red_send.at[2], recv_sem=red_recv.at[2],
            device_id=peer, device_id_type=MESH,
        ).start()

    pltpu.make_async_copy(others, others, red_send.at[0]).wait()
    pltpu.make_async_copy(others_z, others_z, red_send.at[1]).wait()
    others_a = ga.at[pl.ds(0, GROUP - 1)]
    pltpu.make_async_copy(others_a, others_a, red_recv.at[2]).wait()
    pltpu.make_async_copy(others_a, others_a, red_send.at[2]).wait()
    for q in range(GROUP):
        total[2 * q : 2 * q + 2] = ga[q]
    pass_u.wait_recv()
    pass_v.wait_recv()
    for copy in halos + hand:
        copy.wait_send()
    for copy in (up_first, down_first, up_last, down_last, pass_up, pass_down, up_u, down_u, up_v, down_v, pass_u, pass_v):
        copy.wait_send()
    pltpu.make_async_copy(everyone, everyone, tab_send).wait()


def inverse_factor(g):
    sub = lax.broadcasted_iota(jnp.int32, (8, 2 * M), 0)
    lane = lax.broadcasted_iota(jnp.int32, (8, 2 * M), 1)
    work = []
    for n in range(M // 8):
        diagonal = jnp.where(lane == sub + 8 * n, float(M - 1), 0.0)
        right = jnp.where(lane == sub + 8 * n + M, 1.0, 0.0)
        work.append(jnp.where(lane < M, g[8 * n : 8 * n + 8] + diagonal, right))

    spot = lax.broadcasted_iota(jnp.int32, (M, 2 * M), 0) == lax.broadcasted_iota(jnp.int32, (M, 2 * M), 1)
    proj = jnp.where(spot, jnp.broadcast_to(g[:, M : M + 1], (M, 2 * M)), 0.0)
    work.append(jnp.broadcast_to(jnp.sum(proj, axis=0, keepdims=True), (8, 2 * M)))

    def spread(row):
        return jnp.broadcast_to(row, (8, 2 * M))

    result = []
    for n in range(M // 8):
        below = range(n, M // 8 + 1)
        column = [{r: spread(work[r][:, 8 * n + j : 8 * n + j + 1]) for r in below} for j in range(8)]
        pivots = jnp.zeros((8, 2 * M), jnp.float32)
        for j in range(8):
            pivot = spread(column[j][n][j : j + 1])
            pivots = jnp.where(sub == j, pivot, pivots)
            inverse = 1.0 / pivot
            ratio = {r: column[j][r] * inverse for r in below}
            ratio[n] = jnp.where(sub > j, ratio[n], 0.0)
            for k in range(j + 1, 8):
                head = spread(column[k][n][j : j + 1])
                for r in below:
                    column[k][r] = column[k][r] - ratio[r] * head
            row = spread(work[n][j : j + 1])
            for r in below:
                work[r] = work[r] - ratio[r] * row
        result.append(jnp.where(lane >= M, work[n] * (1.0 / jnp.sqrt(pivots)), 0.0))
    return jnp.concatenate(result, axis=0), -work[M // 8][0:1]


def combine_kernel(total, fc, out, inv_ref, held, sem):
    y = lax.axis_index("mem")
    lower_inv, mean_weights = inverse_factor(total[...])
    inv_ref[...] = lower_inv
    coef = mean_weights + math.sqrt(M - 1) * inv_ref[pl.ds(pl.multiple_of(y * LM, LM), LM), :]
    coef = coef[:, M:]
    mixing = coef + (1.0 - jnp.sum(coef, axis=1, keepdims=True)) * (1.0 / M)
    mix_high, mix_low = two_terms(mixing)
    mix = jnp.concatenate([mix_high, mix_high, mix_low], axis=1)
    stores = []
    for f in range(3):

        @pl.loop(0, ROWS, unroll=ROWS)
        def _(r):
            high, low = two_terms(jnp.concatenate([fc[yb, f, r] for yb in range(NM)], axis=0))
            prior = jnp.concatenate([high, low, high], axis=0)
            new = jnp.dot(mix, prior, preferred_element_type=jnp.float32)
            for c in range(2):
                held[2 * f + c, pl.ds(r, LM, stride=ROWS), :] = new[:, c * OBS : (c + 1) * OBS]

        for c in range(2):
            ready = held.at[2 * f + c].reshape(LM, ROWS, OBS)
            stores.append(pltpu.make_async_copy(ready, out.at[:, f, :, pl.ds(c * OBS, OBS)], sem.at[2 * f + c]))
            stores[-1].start()
    for store in stores:
        store.wait()


def local(state, depth, obs_cells, obs_weights, owner_map, obs_values, obs_precision):
    any_space = pl.BlockSpec(memory_space=pltpu.HBM)
    f32 = jnp.float32
    fc, total = pl.pallas_call(
        main_kernel,
        name="forecast_and_reduce",
        out_shape=(
            jax.ShapeDtypeStruct((NM, 3, ROWS, LM, COLS), f32),
            jax.ShapeDtypeStruct((M, 2 * M), f32),
        ),
        in_specs=[any_space] * 7,
        out_specs=(pl.BlockSpec(memory_space=pltpu.VMEM), pl.BlockSpec(memory_space=pltpu.VMEM)),
        scratch_shapes=[
            pltpu.VMEM((1, 8192 // NS), jnp.int32),
            pltpu.VMEM((2, LM * 3 * ROWS, OBS), f32),
            pltpu.VMEM((ROWS, COLS), f32),
            pltpu.VMEM((2, 8, COLS), f32),
            pltpu.VMEM((4, BLK, OBS), jnp.int32),
            pltpu.VMEM((4, BLK, OBS), f32),
            pltpu.VMEM((3, EXT, LM, COLS), f32),
            pltpu.VMEM((EXT, 8, COLS), f32),
            pltpu.VMEM((EXT, LM, COLS), f32),
            pltpu.VMEM((EXT, LM, COLS), f32),
            pltpu.VMEM((EXT, LM, COLS), f32),
            pltpu.VMEM((EXT, LM, COLS), f32),
            pltpu.VMEM((NM, ROWS, 8, COLS), jnp.int32),
            pltpu.VMEM((NM, LM, OBS), f32),
            pltpu.VMEM((NM, BLK, LM, OBS), f32),
            pltpu.VMEM((2 * M, BLK * OBS), jnp.bfloat16),
            pltpu.VMEM((2 * M, BLK * OBS), jnp.bfloat16),
            pltpu.VMEM((NS, 2, 2, OBS), f32),
            pltpu.VMEM((NS, 1, OBS), f32),
            pltpu.VMEM((NM, BLK, OBS), f32),
            pltpu.VMEM((NM, BLK, OBS), f32),
            pltpu.VMEM((GROUP, 2, 2 * M), f32),
            pltpu.VMEM((GROUP, 2, 2 * M), f32),
            pltpu.VMEM((2, 2 * M), f32),
            pltpu.VMEM((NZ, 2, 2 * M), f32),
            pltpu.VMEM((GROUP, 2, 2 * M), f32),
            pltpu.SemaphoreType.DMA((9,)),
            pltpu.SemaphoreType.DMA((2, 3)),
            pltpu.SemaphoreType.DMA((2, 3)),
            pltpu.SemaphoreType.DMA((12,)),
            pltpu.SemaphoreType.DMA((12,)),
            pltpu.SemaphoreType.DMA,
            pltpu.SemaphoreType.DMA,
            pltpu.SemaphoreType.DMA((3,)),
            pltpu.SemaphoreType.DMA((3,)),
            pltpu.SemaphoreType.REGULAR((8,)),
            pltpu.SemaphoreType.DMA((NM,)),
            pltpu.SemaphoreType.DMA((NM,)),
        ],
        compiler_params=pltpu.CompilerParams(collective_id=0, has_side_effects=True, vmem_limit_bytes=40 << 20),
    )(
        *(
            pltpu.with_memory_space_constraint(a, pltpu.HBM)
            for a in (
                owner_map.reshape(1, -1), state.reshape(LM * 3 * ROWS, COLS), depth,
                obs_cells, obs_weights, obs_values, obs_precision,
            )
        )
    )
    vmem = pl.BlockSpec(memory_space=pltpu.VMEM)
    out = pl.pallas_call(
        combine_kernel,
        name="combine_members",
        out_shape=jax.ShapeDtypeStruct((LM, 3, ROWS, COLS), f32),
        in_specs=[vmem, vmem],
        out_specs=any_space,
        scratch_shapes=[
            pltpu.VMEM((M, 2 * M), f32),
            pltpu.VMEM((6, LM * ROWS, OBS), f32),
            pltpu.SemaphoreType.DMA((6,)),
        ],
        compiler_params=pltpu.CompilerParams(vmem_limit_bytes=40 << 20),
    )(total, fc)
    return out


def solution(mesh):
    return jax.shard_map(
        local,
        mesh=mesh,
        in_specs=(
            P("mem", None, "space", None),
            P("space", None),
            P(None, "space", None),
            P(None, "space", None),
            P("space", None),
            P("space", None, None, None),
            P("space", None, None, None),
        ),
        out_specs=P("mem", None, "space", None),
        check_vma=False,
    )
```

```python
import math

import jax
import jax.numpy as jnp
from jax import lax
from jax.experimental import pallas as pl
from jax.experimental.pallas import tpu as pltpu
from jax.sharding import PartitionSpec as P

M = 64
NS = 128
NM = 4
NZ = 16
GROUP = 32
LM = M // NM
ROWS = 16
COLS = 256
HALO = 4
EXT = ROWS + 2 * HALO
BLK = 16
OBS = 128
N_OBS = 8192 * 128
GROUPS = (slice(0, 8), slice(8, 16))
EAST, HEIGHT, NORTH = 0, 1, 2
FIELD = (HEIGHT, EAST, NORTH)
MESH = pl.DeviceIdType.MESH
mass_rate = 0.2
wave_rate = 0.2
turn_rate = 0.1


def east(field):
    return pltpu.roll(field, COLS - 1, 1)


def west(field):
    return pltpu.roll(field, 1, 1)


def height_step(i, keep, S, DB, H1):
    for g in GROUPS:
        flux = DB[i] * S[NORTH, i, g]
        change = DB[i + 1] * S[EAST, i + 1, g] - DB[i - 1] * S[EAST, i - 1, g] + (east(flux) - west(flux))
        H1[i, g] = (S[HEIGHT, i, g] - mass_rate * change) * keep


def wind_step(i, S, H1, U1, V1):
    for g in GROUPS:
        u, v, h = S[EAST, i, g], S[NORTH, i, g], H1[i, g]
        U1[i, g] = u - wave_rate * (H1[i + 1, g] - H1[i - 1, g]) + turn_rate * v
        V1[i, g] = v - wave_rate * (east(h) - west(h)) - turn_rate * u


def second_height(i, keep, DB, H1, U1, V1, H2):
    for g in GROUPS:
        flux = DB[i] * V1[i, g]
        change = DB[i + 1] * U1[i + 1, g] - DB[i - 1] * U1[i - 1, g] + (east(flux) - west(flux))
        H2[i, g] = (H1[i, g] - mass_rate * change) * keep


def pack_block(yb, height, packed, inverse):
    top = lax.fori_loop(
        0, ROWS, lambda r, t: jnp.maximum(t, jnp.abs(height(r))), jnp.zeros((LM, COLS), jnp.float32), unroll=4
    )
    top = jnp.maximum(jnp.max(top, axis=1, keepdims=True), 1e-30)
    scale = 32000.0 / top
    inverse[yb] = jnp.broadcast_to(top * (1.0 / 32000.0), (LM, OBS))

    @pl.loop(0, ROWS, unroll=4)
    def _(r):
        q = jnp.floor(height(r) * scale + 0.5).astype(jnp.int32)
        packed[yb, r] = (q[0:8] << 16) | (q[8:16] & 0xFFFF)


def interpolate(half, span, blocks, packed, inverse, cells, weights, pred):
    @pl.loop(*span)
    def _(b):
        lane, chunk, weight = [], [], []
        for k in range(2):
            cell = jnp.broadcast_to(cells[half * 2 + k, pl.ds(b, 1), :], (8, OBS))
            lane.append(cell & (OBS - 1))
            chunk.append(cell >> 7)
            weight.append(jnp.broadcast_to(weights[half * 2 + k, pl.ds(b, 1), :], (8, OBS)))
        held = [[jnp.zeros((8, OBS), jnp.int32) for _ in blocks] for _ in range(2)]
        for c in range(ROWS * COLS // OBS):
            row, col = c // 2, (c % 2) * OBS
            here = [chunk[k] == c for k in range(2)]
            for g, yb in enumerate(blocks):
                values = packed[yb, row, :, col : col + OBS]
                for k in range(2):
                    found = jnp.take_along_axis(values, lane[k], axis=1, mode="promise_in_bounds")
                    held[k][g] = jnp.where(here[k], found, held[k][g])
        for g, yb in enumerate(blocks):
            high = sum((held[k][g] >> 16).astype(jnp.float32) * weight[k] for k in range(2))
            low = sum(((held[k][g] << 16) >> 16).astype(jnp.float32) * weight[k] for k in range(2))
            part = jnp.concatenate([high, low], axis=0) * inverse[yb]
            pred[yb, b] = part if half == 0 else pred[yb, b] + part


def two_terms(value):
    high = value.astype(jnp.bfloat16)
    return high, (value - high.astype(jnp.float32)).astype(jnp.bfloat16)


def tree_sum(terms):
    while len(terms) > 1:
        terms = [sum(terms[i : i + 2][1:], terms[i]) for i in range(0, len(terms), 2)]
    return terms[0]


def main_kernel(
    owners_hbm, state, depth, cells_hbm, weights_hbm, values, precisions, fc, total,
    owners, st, dp, dp_edge, cells, weights, S, DB, H1, U1, V1, H2, packed, inverse, pred, XH, XL, sent, tab, picked, given, Gs, rs, zs, zb, ga,
    load_sem, halo_send, halo_recv, ag_send, ag_recv, tab_send, tab_recv, red_send, red_recv, round_sem, pick_send, pick_recv,
):
    s = lax.axis_index("space")
    y = lax.axis_index("mem")
    core = s % 2
    z = (s // 2) % NZ
    x = s // (2 * NZ)
    y_low, y_high, y_far = (y + 3) % NM, (y + 1) % NM, (y + 2) % NM
    place = (x * NM + y) * 2 + core
    left, right = (s + NS - 1) % NS, (s + 1) % NS

    def along_z(step):
        return (x * (2 * NZ) + ((z + step + NZ) % NZ) * 2 + core, y)

    def along_x(step):
        return (((x + step + 4) % 4) * (2 * NZ) + z * 2 + core, y)

    def along_y(step):
        return (s, (y + step + NM) % NM)

    partner = (s + 1 - 2 * core, y)

    def beside(dx, dy, dc):
        nx, ny, nc = (x + dx) % 4, (y + dy) % NM, core + dc - 2 * dc * core
        return (nx * NM + ny) * 2 + nc, (nx * (2 * NZ) + z * 2 + nc, ny)

    def hops(k, size):
        return min(k, size - k)

    steps = sorted(
        ((dx, dy, dc) for dx in range(4) for dy in range(NM) for dc in range(2) if (dx, dy, dc) != (0, 0, 0)),
        key=lambda d: -(hops(d[0], 4) + hops(d[1], NM)),
    )
    members = [beside(*step) for step in steps]
    ring = [along_z(k) for k in sorted(range(1, NZ), key=lambda k: -hops(k, NZ))]
    own_rows = pl.ds(pl.multiple_of(y * BLK, BLK), BLK)
    loads = [
        pltpu.make_async_copy(state.at[:, pl.ds(0, OBS)], st.at[0], load_sem.at[0]),
        pltpu.make_async_copy(state.at[:, pl.ds(OBS, OBS)], st.at[1], load_sem.at[1]),
        pltpu.make_async_copy(depth, dp, load_sem.at[2]),
        pltpu.make_async_copy(cells_hbm.at[:, own_rows], cells, load_sem.at[3]),
        pltpu.make_async_copy(weights_hbm.at[:, own_rows], weights, load_sem.at[4]),
        pltpu.make_async_copy(owners_hbm, owners, load_sem.at[5]),
        pltpu.make_async_copy(values.at[0], sent.at[:, 0], load_sem.at[6]),
        pltpu.make_async_copy(precisions.at[0], sent.at[:, 1], load_sem.at[7]),
    ]
    for load in loads:
        load.start()

    barrier = pltpu.get_barrier_semaphore()
    cross = (left + core * (right - left), y)
    near = [partner, cross, along_z(1), along_z(-1), along_x(1), along_x(-1), along_y(1), along_y(-1)]
    for peer in near:
        pl.semaphore_signal(barrier, inc=1, device_id=peer, device_id_type=MESH)

    rounds = [
        (along_z(1), along_z(-1)),
        (along_z(2), along_z(-2)),
        (along_z(4), along_z(-4)),
        (partner,),
        (along_x(1), along_x(-1)),
        (along_x(1), along_x(-1)),
        (along_y(1), along_y(-1)),
        (along_y(1), along_y(-1)),
    ]

    def tell(n):
        for peer in rounds[n]:
            pl.semaphore_signal(round_sem.at[n], inc=1, device_id=peer, device_id_type=MESH)

    def hear(n):
        pl.semaphore_wait(round_sem.at[n], len(rounds[n]))

    for terms in (XH, XL):
        terms[M : 2 * M] = jnp.zeros((M, BLK * OBS), jnp.bfloat16)
    for load in loads[:3]:
        load.wait()

    def stage(rows):
        for f in range(3):
            for r in rows:
                for c in range(2):
                    S[FIELD[f], HALO + r, :, c * OBS : (c + 1) * OBS] = st[c, pl.ds(f * ROWS + r, LM, stride=3 * ROWS), :]

    stage([*range(HALO), *range(ROWS - HALO, ROWS)])
    pl.semaphore_wait(barrier, len(near))

    halos = []
    for n, (peer, src, dst) in enumerate(((left, HALO, HALO + ROWS), (right, ROWS, 0))):
        for k, (buf, lead, skip, rows) in enumerate(
            ((S, (EAST,), 0, HALO), (S, (pl.ds(HEIGHT, 2),), n, HALO - 1))
        ):
            halos.append(
                pltpu.make_async_remote_copy(
                    src_ref=buf.at[(*lead, pl.ds(src + skip, rows))], dst_ref=buf.at[(*lead, pl.ds(dst + skip, rows))],
                    send_sem=halo_send.at[n, k], recv_sem=halo_recv.at[n, k], device_id=(peer, y), device_id_type=MESH,
                )
            )
            halos[-1].start()

    for n, (peer, src) in enumerate(((left, 0), (right, 8))):
        halos.append(
            pltpu.make_async_remote_copy(
                src_ref=dp.at[pl.ds(src, 8)], dst_ref=dp_edge.at[1 - n], send_sem=halo_send.at[n, 2], recv_sem=halo_recv.at[n, 2],
                device_id=(peer, y), device_id_type=MESH,
            )
        )
        halos[-1].start()

    tell(0)
    stage(range(HALO, ROWS - HALO))
    for r in range(ROWS):
        DB[HALO + r] = jnp.broadcast_to(dp[pl.ds(r, 1), :], (8, COLS))

    @pl.loop(HALO + 1, HALO + ROWS - 1, unroll=2)
    def _(i):
        height_step(i, 1.0, S, DB, H1)

    @pl.loop(HALO + 2, HALO + ROWS - 2, unroll=2)
    def _(i):
        wind_step(i, S, H1, U1, V1)

    hear(0)
    tell(1)

    @pl.loop(HALO + 3, HALO + ROWS - 3, unroll=2)
    def _(i):
        second_height(i, 1.0, DB, H1, U1, V1, H2)

    for halo in halos:
        halo.wait_recv()

    inside_low = jnp.where(s > 0, 1.0, 0.0).astype(jnp.float32)
    inside_high = jnp.where(s < NS - 1, 1.0, 0.0).astype(jnp.float32)
    for i in range(HALO):
        DB[i] = jnp.broadcast_to(dp_edge[0, pl.ds(8 - HALO + i, 1), :], (8, COLS)) * inside_low
        DB[HALO + ROWS + i] = jnp.broadcast_to(dp_edge[1, pl.ds(i, 1), :], (8, COLS)) * inside_high
    for i in range(1, 5):
        height_step(i, inside_low if i < HALO else 1.0, S, DB, H1)
        height_step(EXT - 1 - i, inside_high if i < HALO else 1.0, S, DB, H1)
    hear(1)
    tell(2)
    for i in range(2, 6):
        wind_step(i, S, H1, U1, V1)
        wind_step(EXT - 1 - i, S, H1, U1, V1)
    for i in range(3, 7):
        second_height(i, inside_low if i < HALO else 1.0, DB, H1, U1, V1, H2)
        second_height(EXT - 1 - i, inside_high if i < HALO else 1.0, DB, H1, U1, V1, H2)

    def share(src, dst, n, peer):
        copy = pltpu.make_async_remote_copy(
            src_ref=src, dst_ref=dst, send_sem=ag_send.at[n], recv_sem=ag_recv.at[n],
            device_id=(s, peer), device_id_type=MESH,
        )
        copy.start()
        return copy

    half = ROWS // 2
    first, last = pl.ds(0, half), pl.ds(half, half)
    sent_first, sent_last = H2.at[pl.ds(HALO, half)], H2.at[pl.ds(HALO + half, half)]
    up_first = share(sent_first, fc.at[y, 0, first], 0, y_high)
    down_first = share(sent_last, fc.at[y, 0, last], 1, y_low)
    up_last = share(sent_last, fc.at[y, 0, last], 2, y_high)
    down_last = share(sent_first, fc.at[y, 0, first], 3, y_low)

    loads[3].wait()
    loads[4].wait()
    pack_block(y, lambda r: H2[HALO + r], packed, inverse)
    interpolate(0, (0, BLK), [y], packed, inverse, cells, weights, pred)
    hear(2)
    tell(3)
    interpolate(1, (0, BLK // 2), [y], packed, inverse, cells, weights, pred)
    hear(3)
    tell(4)
    interpolate(1, (BLK // 2, BLK), [y], packed, inverse, cells, weights, pred)
    up_first.wait_recv()
    down_first.wait_recv()
    pass_up = share(fc.at[y_low, 0, first], fc.at[y_low, 0, first], 4, y_high)
    pass_down = share(fc.at[y_high, 0, last], fc.at[y_high, 0, last], 5, y_low)
    hear(4)
    tell(5)

    @pl.loop(HALO, HALO + ROWS, unroll=2)
    def _(i):
        u, v, h = U1[i], V1[i], H2[i]
        fc[y, 1, i - HALO] = u - wave_rate * (H2[i + 1] - H2[i - 1]) + turn_rate * v
        fc[y, 2, i - HALO] = v - wave_rate * (east(h) - west(h)) - turn_rate * u

    loads[6].wait()
    loads[7].wait()
    hear(5)
    tell(6)

    kind, slot = y // 2, y % 2

    def row_for(peer):
        return sent.at[peer, kind, pl.ds(slot, 1)]

    own_row = pltpu.make_async_copy(row_for(s), tab.at[s], load_sem.at[8])
    own_row.start()

    columns = [((x + dx) % 4) * (2 * NZ) + nc for dx in (2, 1, 3, 0) for nc in (1 - core, core)]

    def send_row(peer):
        pltpu.make_async_remote_copy(
            src_ref=row_for(peer), dst_ref=tab.at[s], send_sem=tab_send, recv_sem=tab_recv,
            device_id=(peer, y), device_id_type=MESH,
        ).start()

    @pl.loop(0, NZ - 1)
    def _(k):
        step = (k + 1) // 2
        there = (z + NZ // 2 + jnp.where(k % 2 == 1, step, NZ - step)) % NZ
        for column in columns:
            send_row(column + there * 2)

    for column in columns[:-1]:
        send_row(column + z * 2)

    up_last.wait_recv()
    down_last.wait_recv()
    pack_block(y_low, lambda r: fc[y_low, 0, r], packed, inverse)
    pack_block(y_high, lambda r: fc[y_high, 0, r], packed, inverse)
    hear(6)
    tell(7)
    pass_up.wait_recv()
    pass_down.wait_recv()
    up_u = share(fc.at[y, 1], fc.at[y, 1], 6, y_high)
    down_u = share(fc.at[y, 1], fc.at[y, 1], 7, y_low)
    pack_block(y_far, lambda r: fc[y_far, 0, r], packed, inverse)
    rest = [y_low, y_high, y_far]
    interpolate(0, (0, BLK), rest, packed, inverse, cells, weights, pred)
    interpolate(1, (0, BLK // 4), rest, packed, inverse, cells, weights, pred)

    loads[5].wait()
    blocks = 8192 // NS
    across = jnp.broadcast_to(owners[...], (blocks, blocks))
    down_at = lax.broadcasted_iota(jnp.int32, (blocks, blocks), 0)
    across_at = lax.broadcasted_iota(jnp.int32, (blocks, blocks), 1)
    mine_down = jnp.sum(jnp.where(down_at == across_at, across, 0), axis=1, keepdims=True)
    earlier = jnp.where((across == mine_down) & (across_at < down_at), 1, 0)
    slot_down = jnp.sum(earlier, axis=1, keepdims=True)
    wanted = jnp.where(slot_down == slot, mine_down, -1)
    choose = jnp.where(lax.broadcasted_iota(jnp.int32, (blocks, NS), 1) == wanted, 1.0, 0.0).astype(jnp.bfloat16)
    own_row.wait()
    everyone = tab.at[pl.ds(0, NS - 1)]
    pltpu.make_async_copy(everyone, everyone, tab_recv).wait()
    rows = tab[...].reshape(NS, OBS)
    high, low = two_terms(rows)
    left_over = (rows - high.astype(jnp.float32) - low.astype(jnp.float32)).astype(jnp.bfloat16)

    def take(term):
        return jnp.dot(choose, term, preferred_element_type=jnp.float32)

    chosen = take(high) + (take(low) + take(left_over))
    for q in range(NM):
        picked[q] = chosen[q * BLK : (q + 1) * BLK]
    hand = []
    for step in range(1, NM):
        peer = (y + step) % NM
        hand.append(
            pltpu.make_async_remote_copy(
                src_ref=picked.at[peer], dst_ref=given.at[y], send_sem=pick_send.at[step], recv_sem=pick_recv.at[step],
                device_id=(s, peer), device_id_type=MESH,
            )
        )
        hand[-1].start()
    given[y] = picked[y]
    up_v = share(fc.at[y, 2], fc.at[y, 2], 10, y_high)
    down_v = share(fc.at[y, 2], fc.at[y, 2], 11, y_low)
    interpolate(1, (BLK // 4, BLK), rest, packed, inverse, cells, weights, pred)
    hear(7)
    for copy in hand:
        copy.wait_recv()

    scale = math.sqrt((M - 1) / N_OBS)

    def keep_terms(rows, at, value):
        XH[rows, at], XL[rows, at] = two_terms(value)

    @pl.loop(0, BLK)
    def _(b):
        at_block = pl.ds(b, 1)
        seen = given[0, at_block, :] + given[1, at_block, :]
        factor = (given[2, at_block, :] + given[3, at_block, :]) * scale
        parts = [pred[yb, b] for yb in range(NM)]
        middle = jnp.sum(parts[0] + parts[1] + parts[2] + parts[3], axis=0, keepdims=True) * (1.0 / M)
        at = pl.ds(pl.multiple_of(b * OBS, OBS), OBS)
        for yb in range(NM):
            keep_terms(slice(yb * LM, (yb + 1) * LM), at, (parts[yb] - middle) * factor)
        depart = jnp.broadcast_to((seen - middle) * factor, (LM, OBS))
        keep_terms(slice(M, M + LM), at, jnp.where(lax.broadcasted_iota(jnp.int32, (LM, OBS), 0) == 0, depart, 0.0))

    def product(a, b):
        return lax.dot_general(a[0:M], b[...], (((1,), (1,)), ((), ())), preferred_element_type=jnp.float32)

    gram = product(XH, XH) + (product(XH, XL) + product(XL, XH))
    for q in range(GROUP):
        Gs[q] = gram[2 * q : 2 * q + 2]
    for q, peer in members:
        pltpu.make_async_remote_copy(
            src_ref=Gs.at[q], dst_ref=rs.at[place], send_sem=red_send.at[0], recv_sem=red_recv.at[0],
            device_id=peer, device_id_type=MESH,
        ).start()

    rs[place] = Gs[place]

    @pl.loop(0, ROWS, unroll=2)
    def _(r):
        fc[y, 0, r] = H2[HALO + r]

    others = rs.at[pl.ds(0, GROUP - 1)]
    pltpu.make_async_copy(others, others, red_recv.at[0]).wait()
    up_u.wait_recv()
    down_u.wait_recv()
    up_v.wait_recv()
    down_v.wait_recv()
    mine = tree_sum([rs[q] for q in range(GROUP)])
    zs[...] = mine
    zb[z] = mine
    for peer in ring:
        pltpu.make_async_remote_copy(
            src_ref=zs, dst_ref=zb.at[z], send_sem=red_send.at[1], recv_sem=red_recv.at[1],
            device_id=peer, device_id_type=MESH,
        ).start()

    pass_u = share(fc.at[y_low, 1], fc.at[y_low, 1], 8, y_high)
    pass_v = share(fc.at[y_high, 2], fc.at[y_high, 2], 9, y_low)
    others_z = zb.at[pl.ds(0, NZ - 1)]
    pltpu.make_async_copy(others_z, others_z, red_recv.at[1]).wait()
    ga[place] = tree_sum([zb[q] for q in range(NZ)])
    for q, peer in members:
        pltpu.make_async_remote_copy(
            src_ref=ga.at[place], dst_ref=ga.at[place], send_sem=red_send.at[2], recv_sem=red_recv.at[2],
            device_id=peer, device_id_type=MESH,
        ).start()

    pltpu.make_async_copy(others, others, red_send.at[0]).wait()
    pltpu.make_async_copy(others_z, others_z, red_send.at[1]).wait()
    others_a = ga.at[pl.ds(0, GROUP - 1)]
    pltpu.make_async_copy(others_a, others_a, red_recv.at[2]).wait()
    pltpu.make_async_copy(others_a, others_a, red_send.at[2]).wait()
    for q in range(GROUP):
        total[2 * q : 2 * q + 2] = ga[q]
    pass_u.wait_recv()
    pass_v.wait_recv()
    for copy in halos + hand:
        copy.wait_send()
    for copy in (up_first, down_first, up_last, down_last, pass_up, pass_down, up_u, down_u, up_v, down_v, pass_u, pass_v):
        copy.wait_send()
    pltpu.make_async_copy(everyone, everyone, tab_send).wait()


def inverse_factor(g):
    sub = lax.broadcasted_iota(jnp.int32, (8, 2 * M), 0)
    lane = lax.broadcasted_iota(jnp.int32, (8, 2 * M), 1)
    work = []
    for n in range(M // 8):
        diagonal = jnp.where(lane == sub + 8 * n, float(M - 1), 0.0)
        right = jnp.where(lane == sub + 8 * n + M, 1.0, 0.0)
        work.append(jnp.where(lane < M, g[8 * n : 8 * n + 8] + diagonal, right))

    spot = lax.broadcasted_iota(jnp.int32, (M, 2 * M), 0) == lax.broadcasted_iota(jnp.int32, (M, 2 * M), 1)
    proj = jnp.where(spot, jnp.broadcast_to(g[:, M : M + 1], (M, 2 * M)), 0.0)
    work.append(jnp.broadcast_to(jnp.sum(proj, axis=0, keepdims=True), (8, 2 * M)))

    def spread(row):
        return jnp.broadcast_to(row, (8, 2 * M))

    result = []
    for n in range(M // 8):
        below = range(n, M // 8 + 1)
        column = [{r: spread(work[r][:, 8 * n + j : 8 * n + j + 1]) for r in below} for j in range(8)]
        pivots = jnp.zeros((8, 2 * M), jnp.float32)
        for j in range(8):
            pivot = spread(column[j][n][j : j + 1])
            pivots = jnp.where(sub == j, pivot, pivots)
            inverse = 1.0 / pivot
            ratio = {r: column[j][r] * inverse for r in below}
            ratio[n] = jnp.where(sub > j, ratio[n], 0.0)
            for k in range(j + 1, 8):
                head = spread(column[k][n][j : j + 1])
                for r in below:
                    column[k][r] = column[k][r] - ratio[r] * head
            row = spread(work[n][j : j + 1])
            for r in below:
                work[r] = work[r] - ratio[r] * row
        result.append(jnp.where(lane >= M, work[n] * (1.0 / jnp.sqrt(pivots)), 0.0))
    return jnp.concatenate(result, axis=0), -work[M // 8][0:1]


def combine_kernel(total, fc, out, inv_ref, held, sem):
    y = lax.axis_index("mem")
    lower_inv, mean_weights = inverse_factor(total[...])
    inv_ref[...] = lower_inv
    coef = mean_weights + math.sqrt(M - 1) * inv_ref[pl.ds(pl.multiple_of(y * LM, LM), LM), :]
    coef = coef[:, M:]
    mixing = coef + (1.0 - jnp.sum(coef, axis=1, keepdims=True)) * (1.0 / M)
    mix_high, mix_low = two_terms(mixing)
    mix = jnp.concatenate([mix_high, mix_high, mix_low], axis=1)
    stores = []
    for f in range(3):

        @pl.loop(0, ROWS, unroll=ROWS)
        def _(r):
            high, low = two_terms(jnp.concatenate([fc[yb, f, r] for yb in range(NM)], axis=0))
            prior = jnp.concatenate([high, low, high], axis=0)
            new = jnp.dot(mix, prior, preferred_element_type=jnp.float32)
            for c in range(2):
                held[2 * f + c, pl.ds(r, LM, stride=ROWS), :] = new[:, c * OBS : (c + 1) * OBS]

        for c in range(2):
            ready = held.at[2 * f + c].reshape(LM, ROWS, OBS)
            stores.append(pltpu.make_async_copy(ready, out.at[:, f, :, pl.ds(c * OBS, OBS)], sem.at[2 * f + c]))
            stores[-1].start()
    for store in stores:
        store.wait()


def local(state, depth, obs_cells, obs_weights, owner_map, obs_values, obs_precision):
    any_space = pl.BlockSpec(memory_space=pltpu.HBM)
    f32 = jnp.float32
    fc, total = pl.pallas_call(
        main_kernel,
        name="forecast_and_reduce",
        out_shape=(
            jax.ShapeDtypeStruct((NM, 3, ROWS, LM, COLS), f32),
            jax.ShapeDtypeStruct((M, 2 * M), f32),
        ),
        in_specs=[any_space] * 7,
        out_specs=(pl.BlockSpec(memory_space=pltpu.VMEM), pl.BlockSpec(memory_space=pltpu.VMEM)),
        scratch_shapes=[
            pltpu.VMEM((1, 8192 // NS), jnp.int32),
            pltpu.VMEM((2, LM * 3 * ROWS, OBS), f32),
            pltpu.VMEM((ROWS, COLS), f32),
            pltpu.VMEM((2, 8, COLS), f32),
            pltpu.VMEM((4, BLK, OBS), jnp.int32),
            pltpu.VMEM((4, BLK, OBS), f32),
            pltpu.VMEM((3, EXT, LM, COLS), f32),
            pltpu.VMEM((EXT, 8, COLS), f32),
            pltpu.VMEM((EXT, LM, COLS), f32),
            pltpu.VMEM((EXT, LM, COLS), f32),
            pltpu.VMEM((EXT, LM, COLS), f32),
            pltpu.VMEM((EXT, LM, COLS), f32),
            pltpu.VMEM((NM, ROWS, 8, COLS), jnp.int32),
            pltpu.VMEM((NM, LM, OBS), f32),
            pltpu.VMEM((NM, BLK, LM, OBS), f32),
            pltpu.VMEM((2 * M, BLK * OBS), jnp.bfloat16),
            pltpu.VMEM((2 * M, BLK * OBS), jnp.bfloat16),
            pltpu.VMEM((NS, 2, 2, OBS), f32),
            pltpu.VMEM((NS, 1, OBS), f32),
            pltpu.VMEM((NM, BLK, OBS), f32),
            pltpu.VMEM((NM, BLK, OBS), f32),
            pltpu.VMEM((GROUP, 2, 2 * M), f32),
            pltpu.VMEM((GROUP, 2, 2 * M), f32),
            pltpu.VMEM((2, 2 * M), f32),
            pltpu.VMEM((NZ, 2, 2 * M), f32),
            pltpu.VMEM((GROUP, 2, 2 * M), f32),
            pltpu.SemaphoreType.DMA((9,)),
            pltpu.SemaphoreType.DMA((2, 3)),
            pltpu.SemaphoreType.DMA((2, 3)),
            pltpu.SemaphoreType.DMA((12,)),
            pltpu.SemaphoreType.DMA((12,)),
            pltpu.SemaphoreType.DMA,
            pltpu.SemaphoreType.DMA,
            pltpu.SemaphoreType.DMA((3,)),
            pltpu.SemaphoreType.DMA((3,)),
            pltpu.SemaphoreType.REGULAR((8,)),
            pltpu.SemaphoreType.DMA((NM,)),
            pltpu.SemaphoreType.DMA((NM,)),
        ],
        compiler_params=pltpu.CompilerParams(collective_id=0, has_side_effects=True, vmem_limit_bytes=40 << 20),
    )(
        *(
            pltpu.with_memory_space_constraint(a, pltpu.HBM)
            for a in (
                owner_map.reshape(1, -1), state.reshape(LM * 3 * ROWS, COLS), depth,
                obs_cells, obs_weights, obs_values, obs_precision,
            )
        )
    )
    vmem = pl.BlockSpec(memory_space=pltpu.VMEM)
    out = pl.pallas_call(
        combine_kernel,
        name="combine_members",
        out_shape=jax.ShapeDtypeStruct((LM, 3, ROWS, COLS), f32),
        in_specs=[vmem, vmem],
        out_specs=any_space,
        scratch_shapes=[
            pltpu.VMEM((M, 2 * M), f32),
            pltpu.VMEM((6, LM * ROWS, OBS), f32),
            pltpu.SemaphoreType.DMA((6,)),
        ],
        compiler_params=pltpu.CompilerParams(vmem_limit_bytes=40 << 20),
    )(total, fc)
    return out


def solution(mesh):
    return jax.shard_map(
        local,
        mesh=mesh,
        in_specs=(
            P("mem", None, "space", None),
            P("space", None),
            P(None, "space", None),
            P(None, "space", None),
            P("space", None),
            P("space", None, None, None),
            P("space", None, None, None),
        ),
        out_specs=P("mem", None, "space", None),
        check_vma=False,
    )
```
